512 devices in a mesh: row: 16 (over y, core), col: 32 (over x, z).
Axes of the slice: x: 4, y: 8, z: 8, core: 2. Of those that a mesh axis runs over, the one named last changes fastest.
Arguments:
- excitons: float32 [1024, 1024], P('row', 'col'), may hold values from -500 to 500
- valence_energy: float32 [1024], P('row'), may hold values from -3 to -1
- conduction_energy: float32 [1024], P('col'), may hold values from 1 to 3
- psi_valence: float32 [4096, 1024], P('row', 'col'), may hold values from -0.1875 to 0.1875
- psi_conduction: float32 [4096, 1024], P('col', 'row'), may hold values from -0.1875 to 0.1875
- screened: float32 [4096, 4096], P('row', 'col'), may hold values from -0.9 to 0.975, as said below
Outputs:
- next_vector: float32 [1024, 1024], P('row', 'col')
- coefficients: float32 [4], replicated
The draws below stay inside these ranges and needn't reach their ends.
Inputs may be any that keep to these rules, and one draw needn't show every extreme that they name: symmetric: screened[p, p'] = screened[p', p].
All inputs are finite; a program needn't handle non-finite values.
Results may differ from the reference program's by a relative error of at most 0.0003.
Values sent between devices are 32-bit elements; how exact they have to be, the bound alone decides.
No kernel may reach another device: no remote copies, remote signals or barrier semaphores. Data moves between devices by JAX's collectives and lax.ppermute only.
A program may use at most 64 MiB of HBM per device.

```python
import math
import jax
import jax.numpy as jnp
from jax import lax

NV = 1024
NC = 1024
NP = 4096
STEPS = 2


def draw_excitons(key, part):
    base_key = jax.random.fold_in(key, 11)
    key_entries, key_rows, key_cols = jax.random.split(base_key, 3)
    row_scale = 3.0 ** (jnp.arange(NV, dtype=jnp.float32) / NV) * jnp.exp(jax.random.uniform(key_rows, (NV,), jnp.float32, 0.0, math.log(3.2)))
    col_scale = 3.0 ** (jnp.arange(NC, dtype=jnp.float32) / NC) * jnp.exp(jax.random.uniform(key_cols, (NC,), jnp.float32, 0.0, math.log(3.2)))
    entries = jnp.clip(jax.random.normal(key_entries, (NV, NC), jnp.float32), -5.0, 5.0)
    return (entries * row_scale[:, None] * col_scale[None, :]).astype(jnp.float32)


def draw_screened(key, part):
    base_key = jax.random.fold_in(key, 23)
    noise_scale = 0.6 * (NV * NC) ** 0.5 / NP
    smooth_height = 1.2 * NV * NC / (NP * NP)
    places = jnp.arange(NP, dtype=jnp.float32)
    distance = jnp.abs(places[:, None] - places[None, :])
    noise = jnp.clip(jax.random.normal(base_key, (NP, NP), jnp.float32), -4.0, 4.0)
    reach = NP / 8.0
    symmetric = (noise + noise.T) * (1.0 / math.sqrt(2.0))
    smooth = smooth_height * jnp.exp(-distance / reach)
    return (noise_scale * symmetric + smooth).astype(jnp.float32)


def levels(own_key, shape, pieces, smallest, largest):
    level = 1.0
    for axis_at, parts in pieces:
        steps = jax.random.uniform(jax.random.fold_in(jax.random.fold_in(own_key, 6), axis_at), (parts,), jnp.float32, smallest / len(pieces), largest / len(pieces))
        level = level * jnp.repeat(jnp.exp(steps), shape[axis_at] // parts).reshape((-1,) + (1,) * (len(shape) - 1 - axis_at))
    return level


def normal_values(stream_key, shape, deviation, limit, shards=(), kind=jnp.bfloat16):
    array = jax.random.normal(stream_key, shape, jnp.float32) * deviation
    if len(shards) > 0:
        array = levels(stream_key, shape, shards, -0.22, 0.18) * array
    return jnp.clip(array, min=-limit, max=limit).astype(kind)


def setup_inputs(seed: int = 0) -> dict:
    seeds = jax.random.split(jax.random.key(seed), 7)
    return {
        "excitons": draw_excitons(jax.random.fold_in(seeds[6], 71), 0),
        "valence_energy": jnp.clip(-3.0 + 2.0 * jax.random.uniform(seeds[1], (NV,), jnp.float32) ** levels(seeds[1], (NV,), ((0, 16),), -0.2, 0.2), -3.0, -1.0),
        "conduction_energy": jnp.clip(1.0 + 2.0 * jax.random.uniform(seeds[2], (NC,), jnp.float32) ** levels(seeds[2], (NC,), ((0, 32),), -0.2, 0.2), 1.0, 3.0),
        "psi_valence": normal_values(seeds[3], (NP, NV), NV ** -0.5, 0.1875, ((0, 16), (1, 32)), jnp.float32),
        "psi_conduction": normal_values(seeds[4], (NP, NC), NC ** -0.5, 0.1875, ((0, 32), (1, 16)), jnp.float32),
        "screened": draw_screened(jax.random.fold_in(seeds[6], 71), 0),
    }


EPS = 1e-06

def inner(left, right):
    return jnp.sum(left * right) / (NV * NC)

def apply_operator(vector, valence_energy, conduction_energy, psi_valence, psi_conduction, screened):
    high = lax.Precision.HIGHEST
    image = jnp.dot(vector, psi_conduction.T, precision=high)
    points = jnp.dot(psi_valence, image, precision=high)
    weighted = points * screened
    back_valence = jnp.dot(psi_valence.T, weighted, precision=high)
    kernel = jnp.dot(back_valence, psi_conduction, precision=high)
    energy_gap = conduction_energy[None, :] - valence_energy[:, None]
    return energy_gap * vector - kernel

def reference(excitons, valence_energy, conduction_energy, psi_valence, psi_conduction, screened):
    vector = excitons / jnp.sqrt(inner(excitons, excitons) + EPS)
    previous = jnp.zeros_like(vector)
    beta_prev = jnp.zeros((), jnp.float32)
    values = []
    for step in range(STEPS):
        image = apply_operator(vector, valence_energy, conduction_energy, psi_valence, psi_conduction, screened)
        alpha = inner(vector, image)
        residual = image - alpha * vector - beta_prev * previous
        beta = jnp.sqrt(inner(residual, residual) + EPS)
        previous = vector
        vector = residual / beta
        beta_prev = beta
        values.append(alpha)
        values.append(beta)
    return (vector, jnp.stack(values))
```

```python
import jax
import jax.numpy as jnp
from jax import lax
from jax.sharding import Mesh
from jax.sharding import PartitionSpec as P

NV = 1024
NC = 1024
COUNT = NV * NC
COL = ("col_0", "col_1")
ROW = ("row_0", "row_1")
EPS = 1e-06
SHIFT = 4.0
HIGH = lax.Precision.HIGHEST


def exchange(value, axis):
    return lax.all_to_all(value, axis, 0, 0, tiled=True)


def copies(value, axis):
    size = lax.axis_size(axis)
    return exchange(jnp.broadcast_to(value[None], (size, *value.shape)), axis)


def pack(block):
    return jnp.concatenate([block[:16], block[16:]], axis=1)


def unpack(packed):
    return jnp.concatenate([packed[:, :64], packed[:, 64:]], axis=0)


def dot(a, b, dims):
    return lax.dot_general(a, b, (dims, ((), ())), precision=HIGH)


def points_of(gathered, lo, hi):
    return dot(gathered[:, :64], lo, ((0,), (0,))) + dot(gathered[:, 64:], hi, ((0,), (0,)))


def shards(excitons, valence_energy, conduction_energy, psi_valence, psi_conduction, screened):
    x = pack(excitons.T)
    gap = pack(conduction_energy[:, None] - valence_energy[None, :]) - SHIFT
    panel_valence = copies(psi_valence.T, COL).reshape(1024, 256)
    panel_conduction = lax.all_gather(psi_conduction.T, ROW, axis=0, tiled=True)
    halves = panel_conduction.reshape(32, 2, 16, 128)
    lo = halves[:, 0].reshape(512, 128)
    hi = halves[:, 1].reshape(512, 128)

    def middle(image):
        points = dot(panel_valence, image, ((0,), (0,)))
        back = dot(panel_valence, points * screened, ((1,), (0,)))
        back = exchange(back.reshape(16, 64, 128), ROW).sum(axis=0)
        kernel = jnp.concatenate(
            [dot(lo, back, ((1,), (1,))), dot(hi, back, ((1,), (1,)))], axis=1
        )
        return exchange(kernel.reshape(32, 16, 128), COL).sum(axis=0)

    x_rows = copies(x, COL).reshape(512, 128)
    image = lax.all_gather(points_of(x_rows, lo, hi), ROW, axis=0, tiled=True)
    y = gap * x - middle(image)

    y_rows = copies(y, COL).reshape(512, 128)
    sums = jnp.stack(
        [
            jnp.sum(x_rows * x_rows, axis=0),
            jnp.sum(x_rows * y_rows, axis=0),
            jnp.sum(y_rows * y_rows, axis=0),
        ]
    )
    sums = jnp.pad(sums, ((0, 5), (0, 0)))
    message = jnp.concatenate([points_of(y_rows, lo, hi), sums], axis=0)
    arrived = lax.all_gather(message, ROW, axis=0, tiled=True).reshape(16, 72, 128)
    moments = jnp.sum(arrived[:, 64:], axis=(0, 2)) / COUNT
    z = gap * y - middle(arrived[:, :64].reshape(1024, 128))

    inverse = 1.0 / jnp.sqrt(moments[0] + EPS)
    first_norm = moments[0] * inverse * inverse
    first_cross = moments[1] * inverse * inverse
    alpha_1 = first_cross + SHIFT * first_norm
    rest_1 = alpha_1 - SHIFT
    beta_1 = jnp.sqrt(
        moments[2] * inverse * inverse
        - 2.0 * rest_1 * first_cross
        + rest_1 * rest_1 * first_norm
        + EPS
    )
    q_1 = x * inverse
    scale = inverse / beta_1
    q_2 = (y - rest_1 * x) * scale
    u = (z - rest_1 * y) * scale - beta_1 * q_1
    parts = jnp.stack(
        [
            jnp.sum(u * u, axis=0),
            jnp.sum(u * q_2, axis=0),
            jnp.sum(q_2 * q_2, axis=0),
            jnp.sum(q_1 * q_2, axis=0),
        ]
    )
    parts = copies(jnp.pad(parts, ((0, 4), (0, 0))), ROW).sum(axis=0)
    parts = copies(parts, COL).sum(axis=0)
    parts = jnp.sum(parts, axis=1) / COUNT
    uu, uq, qq, oq = parts[0], parts[1], parts[2], parts[3]
    alpha_2 = uq + beta_1 * oq + SHIFT * qq
    rest_2 = alpha_2 - SHIFT
    beta_2 = jnp.sqrt(uu - 2.0 * rest_2 * uq + rest_2 * rest_2 * qq + EPS)
    q_3 = (u - rest_2 * q_2) / beta_2
    return unpack(q_3).T, jnp.stack([alpha_1, beta_1, alpha_2, beta_2])


def solution(mesh):
    finer = Mesh(mesh.devices.reshape(8, 2, 4, 8), ("row_0", "row_1", "col_0", "col_1"))
    placed = (P(ROW, COL), P(ROW), P(COL), P(ROW, COL), P(COL, ROW), P(ROW, COL))
    return jax.shard_map(
        shards, mesh=finer, in_specs=placed, out_specs=(P(ROW, COL), P()), check_vma=False
    )
```

```python
import jax
import jax.numpy as jnp
from jax import lax
from jax.sharding import Mesh
from jax.sharding import PartitionSpec as P

NV = 1024
NC = 1024
COUNT = NV * NC
COL = ("col_0", "col_1")
ROW = ("row_0", "row_1")
EPS = 1e-06
SHIFT = 4.0
HIGH = lax.Precision.HIGHEST


def exchange(value, axis):
    return lax.all_to_all(value, axis, 0, 0, tiled=True)


def copies(value, axis):
    size = lax.axis_size(axis)
    return exchange(jnp.broadcast_to(value[None], (size, *value.shape)), axis)


def pack(block):
    return jnp.concatenate([block[:16], block[16:]], axis=1)


def unpack(packed):
    return jnp.concatenate([packed[:, :64], packed[:, 64:]], axis=0)


def dot(a, b, dims):
    return lax.dot_general(a, b, (dims, ((), ())), precision=HIGH)


def points_of(gathered, lo, hi):
    return dot(gathered[:, :64], lo, ((0,), (0,))) + dot(gathered[:, 64:], hi, ((0,), (0,)))


def shards(excitons, valence_energy, conduction_energy, psi_valence, psi_conduction, screened):
    x = pack(excitons.T)
    gap = pack(conduction_energy[:, None] - valence_energy[None, :]) - SHIFT
    panel_conduction = lax.all_gather(psi_conduction.T, ROW, axis=0, tiled=True)
    halves = panel_conduction.reshape(32, 2, 16, 128)
    lo = halves[:, 0].reshape(512, 128)
    hi = halves[:, 1].reshape(512, 128)

    def middle(image, panel_valence):
        points = dot(panel_valence, image, ((0,), (0,)))
        back = dot(panel_valence, points * screened, ((1,), (0,)))
        back = exchange(back.reshape(16, 64, 128), ROW).sum(axis=0)
        kernel = jnp.concatenate(
            [dot(lo, back, ((1,), (1,))), dot(hi, back, ((1,), (1,)))], axis=1
        )
        return exchange(kernel.reshape(32, 16, 128), COL).sum(axis=0)

    x_rows = copies(x, COL).reshape(512, 128)
    first, own_valence = lax.optimization_barrier((points_of(x_rows, lo, hi), psi_valence.T))
    panel_valence = copies(own_valence, COL).reshape(1024, 256)
    image = lax.all_gather(first, ROW, axis=0, tiled=True)
    y = gap * x - middle(image, panel_valence)

    y_rows = copies(y, COL).reshape(512, 128)
    sums = jnp.stack(
        [
            jnp.sum(x_rows * x_rows, axis=0),
            jnp.sum(x_rows * y_rows, axis=0),
            jnp.sum(y_rows * y_rows, axis=0),
        ]
    )
    sums = jnp.pad(sums, ((0, 5), (0, 0)))
    message = jnp.concatenate([points_of(y_rows, lo, hi), sums], axis=0)
    arrived = lax.all_gather(message, ROW, axis=0, tiled=True).reshape(16, 72, 128)
    moments = jnp.sum(arrived[:, 64:], axis=(0, 2)) / COUNT
    z = gap * y - middle(arrived[:, :64].reshape(1024, 128), panel_valence)

    inverse = 1.0 / jnp.sqrt(moments[0] + EPS)
    first_norm = moments[0] * inverse * inverse
    first_cross = moments[1] * inverse * inverse
    alpha_1 = first_cross + SHIFT * first_norm
    rest_1 = alpha_1 - SHIFT
    beta_1 = jnp.sqrt(
        moments[2] * inverse * inverse
        - 2.0 * rest_1 * first_cross
        + rest_1 * rest_1 * first_norm
        + EPS
    )
    q_1 = x * inverse
    scale = inverse / beta_1
    q_2 = (y - rest_1 * x) * scale
    u = (z - rest_1 * y) * scale - beta_1 * q_1
    parts = jnp.stack(
        [jnp.sum(u * u), jnp.sum(u * q_2), jnp.sum(q_2 * q_2), jnp.sum(q_1 * q_2)]
    )
    parts = jnp.repeat(parts, 32)
    parts = copies(parts, ROW).sum(axis=0)
    parts = copies(parts, COL).sum(axis=0) / COUNT
    uu, uq, qq, oq = parts[0], parts[32], parts[64], parts[96]
    alpha_2 = uq + beta_1 * oq + SHIFT * qq
    rest_2 = alpha_2 - SHIFT
    beta_2 = jnp.sqrt(uu - 2.0 * rest_2 * uq + rest_2 * rest_2 * qq + EPS)
    q_3 = (u - rest_2 * q_2) / beta_2
    return unpack(q_3).T, jnp.stack([alpha_1, beta_1, alpha_2, beta_2])


def solution(mesh):
    finer = Mesh(mesh.devices.reshape(8, 2, 4, 8), ("row_0", "row_1", "col_0", "col_1"))
    placed = (P(ROW, COL), P(ROW), P(COL), P(ROW, COL), P(COL, ROW), P(ROW, COL))
    return jax.shard_map(
        shards, mesh=finer, in_specs=placed, out_specs=(P(ROW, COL), P()), check_vma=False
    )
```

```python
import jax
import jax.numpy as jnp
from jax import lax
from jax.experimental import pallas as pl
from jax.experimental.pallas import tpu as pltpu
from jax.sharding import Mesh
from jax.sharding import PartitionSpec as P

NV = 1024
NC = 1024
COUNT = NV * NC
COL = ("col_0", "col_1")
ROW = ("row_0", "row_1")
EPS = 1e-06
SHIFT = 4.0
HIGH = lax.Precision.HIGHEST
F32 = jnp.float32


def exchange(value, axis):
    return lax.all_to_all(value, axis, 0, 0, tiled=True)


def copies(value, axis):
    size = lax.axis_size(axis)
    return exchange(jnp.broadcast_to(value[None], (size, *value.shape)), axis)


def dot(a, b, left, right):
    return lax.dot_general(
        a, b, (((left,), (right,)), ((), ())), precision=HIGH, preferred_element_type=F32
    )


def call(body, outs, name, smem=()):
    shapes = tuple(jax.ShapeDtypeStruct(s, F32) for s in outs)
    specs = tuple(
        pl.BlockSpec(memory_space=pltpu.SMEM if i in smem else pltpu.VMEM)
        for i in range(len(outs))
    )
    return pl.pallas_call(
        body,
        out_shape=shapes,
        out_specs=specs,
        name=name,
        compiler_params=pltpu.CompilerParams(vmem_limit_bytes=32 * 1024 * 1024),
    )


def start_body(block, packed, spread):
    value = jnp.concatenate([block[0:16, :], block[16:32, :]], axis=1)
    packed[...] = value
    spread[...] = jnp.broadcast_to(value[None], spread.shape)


def points_of(rows, panel):
    lo = dot(rows, panel[:, 0].reshape(512, 128), 0, 0)
    hi = dot(rows, panel[:, 1].reshape(512, 128), 0, 0)
    return lo[0:64] + hi[64:128]


def first_points_body(rows, panel, out):
    out[...] = points_of(rows[...].reshape(512, 128), panel)


def second_points_body(x_rows, y_rows, panel, out):
    x = x_rows[...].reshape(512, 128)
    y = y_rows[...].reshape(512, 128)
    out[0:64, :] = points_of(y, panel)
    out[64:65, :] = jnp.sum(x * x, axis=0, keepdims=True)
    out[65:66, :] = jnp.sum(x * y, axis=0, keepdims=True)
    out[66:67, :] = jnp.sum(y * y, axis=0, keepdims=True)
    out[67:72, :] = jnp.zeros((5, 128), F32)


def weigh(image, panel, screened, out):
    points = dot(panel, image, 0, 0)
    out[...] = dot(panel, points * screened, 1, 0).reshape(16, 64, 128)


def first_weigh_body(image, panel, screened, out):
    weigh(image[...], panel[...], screened[...], out)


def second_weigh_body(arrived, panel, screened, out, moments):
    image = arrived[:, 0:64, :].reshape(1024, 128)
    weigh(image, panel[...], screened[...], out)
    moments[...] = jnp.sum(arrived[:, 64:72, :], axis=0)


def conduct_body(parts, panel, out):
    back = jnp.sum(parts[...], axis=0)
    zero = jnp.zeros_like(back)
    lo = dot(panel[:, 0].reshape(512, 128), jnp.concatenate([back, zero], axis=0), 1, 1)
    hi = dot(panel[:, 1].reshape(512, 128), jnp.concatenate([zero, back], axis=0), 1, 1)
    out[...] = (lo + hi).reshape(32, 16, 128)


def update_body(parts, gap, x, packed, spread):
    value = gap[...] * x[...] - jnp.sum(parts[...], axis=0)
    packed[...] = value
    spread[...] = jnp.broadcast_to(value[None], spread.shape)


def total(value):
    return jnp.sum(jnp.sum(value, axis=0, keepdims=True), axis=1, keepdims=True)


def last_body(parts, gap, x, y, moments, u_out, q_out, message, scalars):
    norm = total(moments[0:1, :]) / COUNT
    inverse = 1.0 / jnp.sqrt(norm + EPS)
    first_norm = norm * inverse * inverse
    first_cross = total(moments[1:2, :]) / COUNT * inverse * inverse
    alpha = first_cross + SHIFT * first_norm
    rest = alpha - SHIFT
    beta = jnp.sqrt(
        total(moments[2:3, :]) / COUNT * inverse * inverse
        - 2.0 * rest * first_cross
        + rest * rest * first_norm
        + EPS
    )
    z = gap[...] * y[...] - jnp.sum(parts[...], axis=0)
    q_1 = x[...] * inverse
    scale = inverse / beta
    q_2 = (y[...] - rest * x[...]) * scale
    u = (z - rest * y[...]) * scale - beta * q_1
    u_out[...] = u
    q_out[...] = q_2
    lane = lax.broadcasted_iota(jnp.int32, (1, 128), 1)
    row = jnp.where(lane < 32, total(u * u), total(u * q_2))
    row = jnp.where(lane < 64, row, jnp.where(lane < 96, total(q_2 * q_2), total(q_1 * q_2)))
    message[...] = jnp.broadcast_to(row[None], message.shape)
    scalars[...] = jnp.where(lane < 64, alpha, beta)


def fold_body(parts, message):
    row = jnp.sum(parts[...], axis=0)
    message[...] = jnp.broadcast_to(row[None], message.shape)


def finish_body(parts, u, q_2, scalars, out, coefficients):
    row = jnp.sum(parts[...], axis=0) / COUNT
    uu, uq, qq, oq = row[:, 0:1], row[:, 32:33], row[:, 64:65], row[:, 96:97]
    beta_1 = scalars[:, 64:65]
    alpha = uq + beta_1 * oq + SHIFT * qq
    rest = alpha - SHIFT
    beta = jnp.sqrt(uu - 2.0 * rest * uq + rest * rest * qq + EPS)
    value = (u[...] - rest * q_2[...]) / beta
    out[0:16, :] = value[:, 0:64]
    out[16:32, :] = value[:, 64:128]
    coefficients[0] = scalars[0, 0]
    coefficients[1] = scalars[0, 64]
    coefficients[2] = alpha[0, 0]
    coefficients[3] = beta[0, 0]


def shards(excitons, valence_energy, conduction_energy, psi_valence, psi_conduction, screened):
    x, spread = call(start_body, [(16, 128), (32, 16, 128)], "start")(excitons.T)
    gap = conduction_energy[:, None] - valence_energy[None, :] - SHIFT
    gap = jnp.concatenate([gap[:16], gap[16:]], axis=1)
    x_rows = exchange(spread, COL)
    panel_valence = copies(psi_valence.T, COL).reshape(1024, 256)
    panel_conduction = lax.all_gather(psi_conduction.T, ROW, axis=0, tiled=True)
    panel_conduction = panel_conduction.reshape(32, 2, 16, 128)

    def returned(back):
        back = exchange(back, ROW)
        (kernel,) = call(conduct_body, [(32, 16, 128)], "conduct")(back, panel_conduction)
        return exchange(kernel, COL)

    (image,) = call(first_points_body, [(64, 128)], "points_one")(x_rows, panel_conduction)
    image = lax.all_gather(image, ROW, axis=0, tiled=True)
    (back,) = call(first_weigh_body, [(16, 64, 128)], "weigh_one")(image, panel_valence, screened)
    y, spread = call(update_body, [(16, 128), (32, 16, 128)], "update")(returned(back), gap, x)

    y_rows = exchange(spread, COL)
    (image,) = call(second_points_body, [(72, 128)], "points_two")(x_rows, y_rows, panel_conduction)
    image = lax.all_gather(image, ROW, axis=0, tiled=True).reshape(16, 72, 128)
    back, moments = call(second_weigh_body, [(16, 64, 128), (8, 128)], "weigh_two")(
        image, panel_valence, screened
    )
    u, q_2, message, scalars = call(
        last_body, [(16, 128), (16, 128), (16, 1, 128), (1, 128)], "last"
    )(returned(back), gap, x, y, moments)
    (message,) = call(fold_body, [(32, 1, 128)], "fold")(exchange(message, ROW))
    out, coefficients = call(finish_body, [(32, 64), (4,)], "finish", smem=(1,))(
        exchange(message, COL), u, q_2, scalars
    )
    return out.T, coefficients


def solution(mesh):
    finer = Mesh(mesh.devices.reshape(8, 2, 4, 8), ("row_0", "row_1", "col_0", "col_1"))
    placed = (P(ROW, COL), P(ROW), P(COL), P(ROW, COL), P(COL, ROW), P(ROW, COL))
    return jax.shard_map(
        shards, mesh=finer, in_specs=placed, out_specs=(P(ROW, COL), P()), check_vma=False
    )
```

```python
import jax
import jax.numpy as jnp
from jax import lax
from jax.experimental import pallas as pl
from jax.experimental.pallas import tpu as pltpu
from jax.sharding import Mesh
from jax.sharding import PartitionSpec as P

NV = 1024
NC = 1024
COUNT = NV * NC
COL = ("col_0", "col_1")
ROW = ("row_0", "row_1")
EPS = 1e-06
SHIFT = 4.0
HIGH = lax.Precision.HIGHEST
F32 = jnp.float32


def exchange(value, axis):
    return lax.all_to_all(value, axis, 0, 0, tiled=True)


def dot(a, b, left, right):
    return lax.dot_general(
        a, b, (((left,), (right,)), ((), ())), precision=HIGH, preferred_element_type=F32
    )


def call(body, outs, name, smem=()):
    shapes = tuple(jax.ShapeDtypeStruct(s, F32) for s in outs)
    specs = tuple(
        pl.BlockSpec(memory_space=pltpu.SMEM if i in smem else pltpu.VMEM)
        for i in range(len(outs))
    )
    return pl.pallas_call(
        body,
        out_shape=shapes,
        out_specs=specs,
        name=name,
        compiler_params=pltpu.CompilerParams(vmem_limit_bytes=32 * 1024 * 1024),
    )


def start_body(block, valence, packed, first, second):
    value = jnp.concatenate([block[0:16, :], block[16:32, :]], axis=1)
    packed[...] = value
    first[:, 0:16, :] = jnp.broadcast_to(value[None], (32, 16, 128))
    first[:, 16:48, :] = jnp.broadcast_to(valence[:, 0:128][None], (32, 32, 128))
    second[...] = jnp.broadcast_to(valence[:, 128:256][None], second.shape)


def points_of(rows, panel):
    lo = dot(rows, panel[:, 0].reshape(512, 128), 0, 0)
    hi = dot(rows, panel[:, 1].reshape(512, 128), 0, 0)
    return lo[0:64] + hi[64:128]


def first_points_body(first, panel, out):
    out[...] = points_of(first[:, 0:16, :].reshape(512, 128), panel)


def second_points_body(first, y_rows, panel, out):
    x = first[:, 0:16, :].reshape(512, 128)
    y = y_rows[...].reshape(512, 128)
    out[0:64, :] = points_of(y, panel)
    out[64:65, :] = jnp.sum(x * x, axis=0, keepdims=True)
    out[65:66, :] = jnp.sum(x * y, axis=0, keepdims=True)
    out[66:67, :] = jnp.sum(y * y, axis=0, keepdims=True)
    out[67:72, :] = jnp.zeros((5, 128), F32)


def weigh(image, first, second, screened, out):
    panel = jnp.concatenate(
        [first[:, 16:48, :].reshape(1024, 128), second[...].reshape(1024, 128)], axis=1
    )
    points = dot(image.T, panel, 1, 0).T
    out[...] = dot(panel, points * screened[...], 1, 0).reshape(16, 64, 128)


def first_weigh_body(image, first, second, screened, out):
    weigh(image[...], first, second, screened, out)


def second_weigh_body(arrived, first, second, screened, out, moments):
    weigh(arrived[:, 0:64, :].reshape(1024, 128), first, second, screened, out)
    moments[...] = jnp.sum(arrived[:, 64:72, :], axis=0)


def conduct_body(parts, panel, out):
    back = jnp.sum(parts[...], axis=0)
    zero = jnp.zeros_like(back)
    lo = dot(panel[:, 0].reshape(512, 128), jnp.concatenate([back, zero], axis=0), 1, 1)
    hi = dot(panel[:, 1].reshape(512, 128), jnp.concatenate([zero, back], axis=0), 1, 1)
    out[...] = (lo + hi).reshape(32, 16, 128)


def update_body(parts, valence, conduction, x, packed, spread, gap_out):
    rows = lax.broadcasted_iota(jnp.int32, (32, 32), 0)
    lanes = lax.broadcasted_iota(jnp.int32, (32, 32), 1)
    column = jnp.sum(jnp.where(rows == lanes, conduction[...], 0.0), axis=1, keepdims=True)
    half = lax.broadcasted_iota(jnp.int32, (16, 128), 1) < 64
    upper = jnp.where(half, column[0:16], column[16:32])
    gap = upper - jnp.concatenate([valence[...], valence[...]], axis=1) - SHIFT
    gap_out[...] = gap
    value = gap * x[...] - jnp.sum(parts[...], axis=0)
    packed[...] = value
    spread[...] = jnp.broadcast_to(value[None], spread.shape)


def total(value):
    return jnp.sum(jnp.sum(value, axis=0, keepdims=True), axis=1, keepdims=True)


def last_body(parts, gap, x, y, moments, u_out, q_out, message, scalars):
    norm = total(moments[0:1, :]) / COUNT
    inverse = 1.0 / jnp.sqrt(norm + EPS)
    first_norm = norm * inverse * inverse
    first_cross = total(moments[1:2, :]) / COUNT * inverse * inverse
    alpha = first_cross + SHIFT * first_norm
    rest = alpha - SHIFT
    beta = jnp.sqrt(
        total(moments[2:3, :]) / COUNT * inverse * inverse
        - 2.0 * rest * first_cross
        + rest * rest * first_norm
        + EPS
    )
    z = gap[...] * y[...] - jnp.sum(parts[...], axis=0)
    q_1 = x[...] * inverse
    scale = inverse / beta
    q_2 = (y[...] - rest * x[...]) * scale
    u = (z - rest * y[...]) * scale - beta * q_1
    u_out[...] = u
    q_out[...] = q_2
    lane = lax.broadcasted_iota(jnp.int32, (1, 128), 1)
    row = jnp.where(lane < 32, total(u * u), total(u * q_2))
    row = jnp.where(lane < 64, row, jnp.where(lane < 96, total(q_2 * q_2), total(q_1 * q_2)))
    message[...] = jnp.broadcast_to(row[None], message.shape)
    scalars[...] = jnp.where(lane < 64, alpha, beta)


def fold_body(parts, message):
    row = jnp.sum(parts[...], axis=0)
    message[...] = jnp.broadcast_to(row[None], message.shape)


def finish_body(parts, u, q_2, scalars, out, coefficients):
    row = jnp.sum(parts[...], axis=0) / COUNT
    uu, uq, qq, oq = row[:, 0:1], row[:, 32:33], row[:, 64:65], row[:, 96:97]
    beta_1 = scalars[:, 64:65]
    alpha = uq + beta_1 * oq + SHIFT * qq
    rest = alpha - SHIFT
    beta = jnp.sqrt(uu - 2.0 * rest * uq + rest * rest * qq + EPS)
    value = (u[...] - rest * q_2[...]) / beta
    out[0:16, :] = value[:, 0:64]
    out[16:32, :] = value[:, 64:128]
    coefficients[0] = scalars[0, 0]
    coefficients[1] = scalars[0, 64]
    coefficients[2] = alpha[0, 0]
    coefficients[3] = beta[0, 0]


def shards(excitons, valence_energy, conduction_energy, psi_valence, psi_conduction, screened):
    x, first, second = call(start_body, [(16, 128), (32, 48, 128), (32, 32, 128)], "start")(
        excitons.T, psi_valence.T
    )
    first = exchange(first, COL)
    panel_conduction = lax.all_gather(psi_conduction.T, ROW, axis=0, tiled=True)
    panel_conduction = panel_conduction.reshape(32, 2, 16, 128)

    def returned(back):
        back = exchange(back, ROW)
        (kernel,) = call(conduct_body, [(32, 16, 128)], "conduct")(back, panel_conduction)
        return exchange(kernel, COL)

    (image,) = call(first_points_body, [(64, 128)], "points_one")(first, panel_conduction)
    image, second = lax.optimization_barrier((image, second))
    second = exchange(second, COL)
    image = lax.all_gather(image, ROW, axis=0, tiled=True)
    (back,) = call(first_weigh_body, [(16, 64, 128)], "weigh_one")(image, first, second, screened)
    y, spread, gap = call(update_body, [(16, 128), (32, 16, 128), (16, 128)], "update")(
        returned(back), valence_energy[None], conduction_energy[None], x
    )

    y_rows = exchange(spread, COL)
    (image,) = call(second_points_body, [(72, 128)], "points_two")(first, y_rows, panel_conduction)
    image = lax.all_gather(image, ROW, axis=0, tiled=True).reshape(16, 72, 128)
    back, moments = call(second_weigh_body, [(16, 64, 128), (8, 128)], "weigh_two")(
        image, first, second, screened
    )
    u, q_2, message, scalars = call(
        last_body, [(16, 128), (16, 128), (16, 1, 128), (1, 128)], "last"
    )(returned(back), gap, x, y, moments)
    (message,) = call(fold_body, [(32, 1, 128)], "fold")(exchange(message, ROW))
    out, coefficients = call(finish_body, [(32, 64), (4,)], "finish", smem=(1,))(
        exchange(message, COL), u, q_2, scalars
    )
    return out.T, coefficients


def solution(mesh):
    finer = Mesh(mesh.devices.reshape(8, 2, 4, 8), ("row_0", "row_1", "col_0", "col_1"))
    placed = (P(ROW, COL), P(ROW), P(COL), P(ROW, COL), P(COL, ROW), P(ROW, COL))
    return jax.shard_map(
        shards, mesh=finer, in_specs=placed, out_specs=(P(ROW, COL), P()), check_vma=False
    )
```

```python
import jax
import jax.numpy as jnp
from jax import lax
from jax.experimental import pallas as pl
from jax.experimental.pallas import tpu as pltpu
from jax.sharding import Mesh
from jax.sharding import PartitionSpec as P

NV = 1024
NC = 1024
COUNT = NV * NC
COL = ("col_0", "col_1")
ROW = ("row_0", "row_1")
EPS = 1e-06
SHIFT = 4.0
HIGH = lax.Precision.HIGHEST
F32 = jnp.float32


def exchange(value, axis):
    return lax.all_to_all(value, axis, 0, 0, tiled=True)


def dot(a, b, left, right):
    return lax.dot_general(
        a, b, (((left,), (right,)), ((), ())), precision=HIGH, preferred_element_type=F32
    )


def halves(value):
    upper = value.astype(jnp.bfloat16)
    return upper, (value - upper.astype(F32)).astype(jnp.bfloat16)


def dot_halves(a, b):
    (a_hi, a_lo), (b_hi, b_lo) = a, b
    return (
        jnp.dot(a_lo, b_hi, preferred_element_type=F32)
        + jnp.dot(a_hi, b_lo, preferred_element_type=F32)
        + jnp.dot(a_hi, b_hi, preferred_element_type=F32)
    )


def call(body, outs, name, smem=()):
    shapes = tuple(jax.ShapeDtypeStruct(s, F32) for s in outs)
    specs = tuple(
        pl.BlockSpec(memory_space=pltpu.SMEM if i in smem else pltpu.VMEM)
        for i in range(len(outs))
    )
    return pl.pallas_call(
        body,
        out_shape=shapes,
        out_specs=specs,
        name=name,
        compiler_params=pltpu.CompilerParams(vmem_limit_bytes=32 * 1024 * 1024),
    )


def start_body(
    block_in, panel_in, valence_in, conduction_in, packed, gap, first, second,
    block, panel, valence, conduction, arrived,
):
    moves = [
        pltpu.make_async_copy(source, target, arrived.at[i])
        for i, (source, target) in enumerate(
            [
                (block_in, block),
                (panel_in, panel),
                (valence_in, valence),
                (conduction_in, conduction),
            ]
        )
    ]
    for move in moves:
        move.start()
    for move in moves:
        move.wait()
    value = jnp.concatenate([block[0:16, :], block[16:32, :]], axis=1)
    packed[...] = value
    first[:, 0:16, :] = jnp.broadcast_to(value[None], (32, 16, 128))
    first[:, 16:48, :] = jnp.broadcast_to(panel[:, 0:128][None], (32, 32, 128))
    second[...] = jnp.broadcast_to(panel[:, 128:256][None], second.shape)
    rows = lax.broadcasted_iota(jnp.int32, (32, 32), 0)
    lanes = lax.broadcasted_iota(jnp.int32, (32, 32), 1)
    column = jnp.sum(jnp.where(rows == lanes, conduction[...], 0.0), axis=1, keepdims=True)
    half = lax.broadcasted_iota(jnp.int32, (16, 128), 1) < 64
    upper = jnp.where(half, column[0:16], column[16:32])
    gap[...] = upper - jnp.concatenate([valence[...], valence[...]], axis=1) - SHIFT


def points_of(rows, panel):
    lo = dot(rows, panel[:, 0].reshape(512, 128), 0, 0)
    hi = dot(rows, panel[:, 1].reshape(512, 128), 0, 0)
    return lo[0:64] + hi[64:128]


def first_points_body(first, panel, out):
    out[...] = points_of(first[:, 0:16, :].reshape(512, 128), panel)


def second_points_body(first, y_rows, panel, out):
    x = first[:, 0:16, :].reshape(512, 128)
    y = y_rows[...].reshape(512, 128)
    out[0:64, :] = points_of(y, panel)
    out[64:65, :] = jnp.sum(x * x, axis=0, keepdims=True)
    out[65:66, :] = jnp.sum(x * y, axis=0, keepdims=True)
    out[66:67, :] = jnp.sum(y * y, axis=0, keepdims=True)
    out[67:72, :] = jnp.zeros((5, 128), F32)


def weigh(image, first, second, screened, out):
    panel = jnp.concatenate(
        [first[:, 16:48, :].reshape(1024, 128), second[...].reshape(1024, 128)], axis=1
    )
    panel = halves(panel)
    points = dot_halves(halves(image.T), panel).T
    out[...] = dot_halves(panel, halves(points * screened[...])).reshape(16, 64, 128)


def first_weigh_body(image, first, second, screened, out):
    weigh(image[...], first, second, screened, out)


def second_weigh_body(arrived, first, second, screened, out, moments):
    weigh(arrived[:, 0:64, :].reshape(1024, 128), first, second, screened, out)
    moments[...] = jnp.sum(arrived[:, 64:72, :], axis=0)


def conduct_body(parts, panel, out):
    back = jnp.sum(parts[...], axis=0)
    zero = jnp.zeros_like(back)
    lo = dot(panel[:, 0].reshape(512, 128), jnp.concatenate([back, zero], axis=0), 1, 1)
    hi = dot(panel[:, 1].reshape(512, 128), jnp.concatenate([zero, back], axis=0), 1, 1)
    out[...] = (lo + hi).reshape(32, 16, 128)


def update_body(parts, gap, x, packed, spread):
    value = gap[...] * x[...] - jnp.sum(parts[...], axis=0)
    packed[...] = value
    spread[...] = jnp.broadcast_to(value[None], spread.shape)


def total(value):
    return jnp.sum(jnp.sum(value, axis=0, keepdims=True), axis=1, keepdims=True)


def last_body(parts, gap, x, y, moments, u_out, q_out, message, scalars):
    norm = total(moments[0:1, :]) / COUNT
    inverse = 1.0 / jnp.sqrt(norm + EPS)
    first_norm = norm * inverse * inverse
    first_cross = total(moments[1:2, :]) / COUNT * inverse * inverse
    alpha = first_cross + SHIFT * first_norm
    rest = alpha - SHIFT
    beta = jnp.sqrt(
        total(moments[2:3, :]) / COUNT * inverse * inverse
        - 2.0 * rest * first_cross
        + rest * rest * first_norm
        + EPS
    )
    z = gap[...] * y[...] - jnp.sum(parts[...], axis=0)
    q_1 = x[...] * inverse
    scale = inverse / beta
    q_2 = (y[...] - rest * x[...]) * scale
    u = (z - rest * y[...]) * scale - beta * q_1
    u_out[...] = u
    q_out[...] = q_2
    lane = lax.broadcasted_iota(jnp.int32, (1, 128), 1)
    row = jnp.where(lane < 32, total(u * u), total(u * q_2))
    row = jnp.where(lane < 64, row, jnp.where(lane < 96, total(q_2 * q_2), total(q_1 * q_2)))
    message[...] = jnp.broadcast_to(row[None], message.shape)
    scalars[...] = jnp.where(lane < 64, alpha, beta)


def fold_body(parts, message):
    row = jnp.sum(parts[...], axis=0)
    message[...] = jnp.broadcast_to(row[None], message.shape)


def finish_body(parts, u, q_2, scalars, out, coefficients):
    row = jnp.sum(parts[...], axis=0) / COUNT
    uu, uq, qq, oq = row[:, 0:1], row[:, 32:33], row[:, 64:65], row[:, 96:97]
    beta_1 = scalars[:, 64:65]
    alpha = uq + beta_1 * oq + SHIFT * qq
    rest = alpha - SHIFT
    beta = jnp.sqrt(uu - 2.0 * rest * uq + rest * rest * qq + EPS)
    value = (u[...] - rest * q_2[...]) / beta
    out[0:16, :] = value[:, 0:64]
    out[16:32, :] = value[:, 64:128]
    coefficients[0] = scalars[0, 0]
    coefficients[1] = scalars[0, 64]
    coefficients[2] = alpha[0, 0]
    coefficients[3] = beta[0, 0]


def shards(excitons, valence_energy, conduction_energy, psi_valence, psi_conduction, screened):
    x, gap, first, second = pl.pallas_call(
        start_body,
        out_shape=tuple(
            jax.ShapeDtypeStruct(shape, F32)
            for shape in [(16, 128), (16, 128), (32, 48, 128), (32, 32, 128)]
        ),
        in_specs=[pl.BlockSpec(memory_space=pltpu.HBM)] * 4,
        out_specs=(pl.BlockSpec(memory_space=pltpu.VMEM),) * 4,
        scratch_shapes=[
            pltpu.VMEM((32, 64), F32),
            pltpu.VMEM((32, 256), F32),
            pltpu.VMEM((1, 64), F32),
            pltpu.VMEM((1, 32), F32),
            pltpu.SemaphoreType.DMA((4,)),
        ],
        name="start",
        compiler_params=pltpu.CompilerParams(vmem_limit_bytes=32 * 1024 * 1024),
    )(
        *(
            pltpu.with_memory_space_constraint(value, pltpu.HBM)
            for value in (
                excitons.T,
                psi_valence.T,
                valence_energy[None],
                conduction_energy[None],
            )
        )
    )
    first = exchange(first, COL)
    panel_conduction = lax.all_gather(psi_conduction.T, ROW, axis=0, tiled=True)
    panel_conduction = panel_conduction.reshape(32, 2, 16, 128)

    def returned(back):
        back = exchange(back, ROW)
        (kernel,) = call(conduct_body, [(32, 16, 128)], "conduct")(back, panel_conduction)
        return exchange(kernel, COL)

    (image,) = call(first_points_body, [(64, 128)], "points_one")(first, panel_conduction)
    image, second = lax.optimization_barrier((image, second))
    second = exchange(second, COL)
    image = lax.all_gather(image, ROW, axis=0, tiled=True)
    (back,) = call(first_weigh_body, [(16, 64, 128)], "weigh_one")(image, first, second, screened)
    y, spread = call(update_body, [(16, 128), (32, 16, 128)], "update")(returned(back), gap, x)

    y_rows = exchange(spread, COL)
    (image,) = call(second_points_body, [(72, 128)], "points_two")(first, y_rows, panel_conduction)
    image = lax.all_gather(image, ROW, axis=0, tiled=True).reshape(16, 72, 128)
    back, moments = call(second_weigh_body, [(16, 64, 128), (8, 128)], "weigh_two")(
        image, first, second, screened
    )
    u, q_2, message, scalars = call(
        last_body, [(16, 128), (16, 128), (16, 1, 128), (1, 128)], "last"
    )(returned(back), gap, x, y, moments)
    (message,) = call(fold_body, [(32, 1, 128)], "fold")(exchange(message, ROW))
    out, coefficients = call(finish_body, [(32, 64), (4,)], "finish", smem=(1,))(
        exchange(message, COL), u, q_2, scalars
    )
    return out.T, coefficients


def solution(mesh):
    finer = Mesh(mesh.devices.reshape(8, 2, 4, 8), ("row_0", "row_1", "col_0", "col_1"))
    placed = (P(ROW, COL), P(ROW), P(COL), P(ROW, COL), P(COL, ROW), P(ROW, COL))
    return jax.shard_map(
        shards, mesh=finer, in_specs=placed, out_specs=(P(ROW, COL), P()), check_vma=False
    )
```

```python
import jax
import jax.numpy as jnp
from jax import lax
from jax.experimental import pallas as pl
from jax.experimental.pallas import tpu as pltpu
from jax.sharding import Mesh
from jax.sharding import PartitionSpec as P

NV = 1024
NC = 1024
COUNT = NV * NC
COL = ("col_0", "col_1")
ROW = ("row_0", "row_1")
EPS = 1e-06
SHIFT = 4.0
HIGH = lax.Precision.HIGHEST
F32 = jnp.float32


def exchange(value, axis):
    return lax.all_to_all(value, axis, 0, 0, tiled=True)


def dot(a, b, left, right):
    return lax.dot_general(
        a, b, (((left,), (right,)), ((), ())), precision=HIGH, preferred_element_type=F32
    )


def halves(value):
    upper = value.astype(jnp.bfloat16)
    return upper, (value - upper.astype(F32)).astype(jnp.bfloat16)


def dot_halves(a, b):
    (a_hi, a_lo), (b_hi, b_lo) = a, b
    return (
        jnp.dot(a_lo, b_hi, preferred_element_type=F32)
        + jnp.dot(a_hi, b_lo, preferred_element_type=F32)
        + jnp.dot(a_hi, b_hi, preferred_element_type=F32)
    )


def call(body, outs, name, smem=()):
    shapes = tuple(jax.ShapeDtypeStruct(s, F32) for s in outs)
    specs = tuple(
        pl.BlockSpec(memory_space=pltpu.SMEM if i in smem else pltpu.VMEM)
        for i in range(len(outs))
    )
    return pl.pallas_call(
        body,
        out_shape=shapes,
        out_specs=specs,
        name=name,
        compiler_params=pltpu.CompilerParams(vmem_limit_bytes=32 * 1024 * 1024),
    )


def start_body(
    block_in, panel_in, valence_in, conduction_in, packed, gap, first, second,
    block, panel, valence, conduction, arrived,
):
    moves = [
        pltpu.make_async_copy(source, target, arrived.at[i])
        for i, (source, target) in enumerate(
            [
                (block_in, block),
                (panel_in, panel),
                (valence_in, valence),
                (conduction_in, conduction),
            ]
        )
    ]
    for move in moves:
        move.start()
    for move in moves:
        move.wait()
    value = jnp.concatenate([block[0:16, :], block[16:32, :]], axis=1)
    packed[...] = value
    first[:, 0:16, :] = jnp.broadcast_to(value[None], (32, 16, 128))
    first[:, 16:48, :] = jnp.broadcast_to(panel[:, 0:128][None], (32, 32, 128))
    second[...] = jnp.broadcast_to(panel[:, 128:256][None], second.shape)
    rows = lax.broadcasted_iota(jnp.int32, (32, 32), 0)
    lanes = lax.broadcasted_iota(jnp.int32, (32, 32), 1)
    column = jnp.sum(jnp.where(rows == lanes, conduction[...], 0.0), axis=1, keepdims=True)
    half = lax.broadcasted_iota(jnp.int32, (16, 128), 1) < 64
    upper = jnp.where(half, column[0:16], column[16:32])
    gap[...] = upper - jnp.concatenate([valence[...], valence[...]], axis=1) - SHIFT


def points_of(rows, panel):
    lo = dot(rows, panel[:, 0].reshape(512, 128), 0, 0)
    hi = dot(rows, panel[:, 1].reshape(512, 128), 0, 0)
    return lo[0:64] + hi[64:128]


def first_points_body(first, panel, out):
    out[...] = points_of(first[:, 0:16, :].reshape(512, 128), panel)


def second_points_body(first, y_rows, panel, out):
    x = first[:, 0:16, :].reshape(512, 128)
    y = y_rows[...].reshape(512, 128)
    out[0:64, :] = points_of(y, panel)
    out[64:65, :] = jnp.sum(x * x, axis=0, keepdims=True)
    out[65:66, :] = jnp.sum(x * y, axis=0, keepdims=True)
    out[66:67, :] = jnp.sum(y * y, axis=0, keepdims=True)
    out[67:72, :] = jnp.zeros((5, 128), F32)


def weigh(image, first, second, screened, out):
    panel = jnp.concatenate(
        [first[:, 16:48, :].reshape(1024, 128), second[...].reshape(1024, 128)], axis=1
    )
    panel = halves(panel)
    points = dot_halves(halves(image.T), panel).T
    back = dot_halves(panel, halves(points * screened[...])).reshape(8, 2, 64, 128)
    out[0] = back[:, 0]
    out[1] = back[:, 1]


def first_weigh_body(image, first, second, screened, out):
    weigh(image[...], first, second, screened, out)


def second_weigh_body(arrived, first, second, screened, out, moments):
    weigh(arrived[:, 0:64, :].reshape(1024, 128), first, second, screened, out)
    moments[...] = jnp.sum(arrived[:, 64:72, :], axis=0)


def pair_body(parts, out):
    out[...] = parts[0] + parts[1]


def conduct_body(parts, panel, out):
    back = jnp.sum(parts[...], axis=0)
    zero = jnp.zeros_like(back)
    lo = dot(panel[:, 0].reshape(512, 128), jnp.concatenate([back, zero], axis=0), 1, 1)
    hi = dot(panel[:, 1].reshape(512, 128), jnp.concatenate([zero, back], axis=0), 1, 1)
    out[...] = (lo + hi).reshape(32, 16, 128)


def update_body(parts, gap, x, packed, spread):
    value = gap[...] * x[...] - jnp.sum(parts[...], axis=0)
    packed[...] = value
    spread[...] = jnp.broadcast_to(value[None], spread.shape)


def total(value):
    return jnp.sum(jnp.sum(value, axis=0, keepdims=True), axis=1, keepdims=True)


def last_body(parts, gap, x, y, moments, u_out, q_out, message, scalars):
    norm = total(moments[0:1, :]) / COUNT
    inverse = 1.0 / jnp.sqrt(norm + EPS)
    first_norm = norm * inverse * inverse
    first_cross = total(moments[1:2, :]) / COUNT * inverse * inverse
    alpha = first_cross + SHIFT * first_norm
    rest = alpha - SHIFT
    beta = jnp.sqrt(
        total(moments[2:3, :]) / COUNT * inverse * inverse
        - 2.0 * rest * first_cross
        + rest * rest * first_norm
        + EPS
    )
    z = gap[...] * y[...] - jnp.sum(parts[...], axis=0)
    q_1 = x[...] * inverse
    scale = inverse / beta
    q_2 = (y[...] - rest * x[...]) * scale
    u = (z - rest * y[...]) * scale - beta * q_1
    u_out[...] = u
    q_out[...] = q_2
    lane = lax.broadcasted_iota(jnp.int32, (1, 128), 1)
    row = jnp.where(lane < 32, total(u * u), total(u * q_2))
    row = jnp.where(lane < 64, row, jnp.where(lane < 96, total(q_2 * q_2), total(q_1 * q_2)))
    message[...] = jnp.broadcast_to(row[None], message.shape)
    scalars[...] = jnp.where(lane < 64, alpha, beta)


def fold_body(parts, message):
    row = jnp.sum(parts[...], axis=0)
    message[...] = jnp.broadcast_to(row[None], message.shape)


def finish_body(parts, u, q_2, scalars, out, coefficients):
    row = jnp.sum(parts[...], axis=0) / COUNT
    uu, uq, qq, oq = row[:, 0:1], row[:, 32:33], row[:, 64:65], row[:, 96:97]
    beta_1 = scalars[:, 64:65]
    alpha = uq + beta_1 * oq + SHIFT * qq
    rest = alpha - SHIFT
    beta = jnp.sqrt(uu - 2.0 * rest * uq + rest * rest * qq + EPS)
    value = (u[...] - rest * q_2[...]) / beta
    out[0:16, :] = value[:, 0:64]
    out[16:32, :] = value[:, 64:128]
    coefficients[0] = scalars[0, 0]
    coefficients[1] = scalars[0, 64]
    coefficients[2] = alpha[0, 0]
    coefficients[3] = beta[0, 0]


def shards(excitons, valence_energy, conduction_energy, psi_valence, psi_conduction, screened):
    x, gap, first, second = pl.pallas_call(
        start_body,
        out_shape=tuple(
            jax.ShapeDtypeStruct(shape, F32)
            for shape in [(16, 128), (16, 128), (32, 48, 128), (32, 32, 128)]
        ),
        in_specs=[pl.BlockSpec(memory_space=pltpu.HBM)] * 4,
        out_specs=(pl.BlockSpec(memory_space=pltpu.VMEM),) * 4,
        scratch_shapes=[
            pltpu.VMEM((32, 64), F32),
            pltpu.VMEM((32, 256), F32),
            pltpu.VMEM((1, 64), F32),
            pltpu.VMEM((1, 32), F32),
            pltpu.SemaphoreType.DMA((4,)),
        ],
        name="start",
        compiler_params=pltpu.CompilerParams(vmem_limit_bytes=32 * 1024 * 1024),
    )(
        *(
            pltpu.with_memory_space_constraint(value, pltpu.HBM)
            for value in (
                excitons.T,
                psi_valence.T,
                valence_energy[None],
                conduction_energy[None],
            )
        )
    )
    first = exchange(first, COL)
    panel_conduction = lax.all_gather(psi_conduction.T, ROW, axis=0, tiled=True)
    panel_conduction = panel_conduction.reshape(32, 2, 16, 128)

    def returned(back):
        (back,) = call(pair_body, [(8, 64, 128)], "pair")(exchange(back, "row_1"))
        back = exchange(back, "row_0")
        (kernel,) = call(conduct_body, [(32, 16, 128)], "conduct")(back, panel_conduction)
        return exchange(kernel, COL)

    (image,) = call(first_points_body, [(64, 128)], "points_one")(first, panel_conduction)
    image, second = lax.optimization_barrier((image, second))
    second = exchange(second, COL)
    image = lax.all_gather(image, ROW, axis=0, tiled=True)
    (back,) = call(first_weigh_body, [(2, 8, 64, 128)], "weigh_one")(image, first, second, screened)
    y, spread = call(update_body, [(16, 128), (32, 16, 128)], "update")(returned(back), gap, x)

    y_rows = exchange(spread, COL)
    (image,) = call(second_points_body, [(72, 128)], "points_two")(first, y_rows, panel_conduction)
    image = lax.all_gather(image, ROW, axis=0, tiled=True).reshape(16, 72, 128)
    back, moments = call(second_weigh_body, [(2, 8, 64, 128), (8, 128)], "weigh_two")(
        image, first, second, screened
    )
    u, q_2, message, scalars = call(
        last_body, [(16, 128), (16, 128), (16, 1, 128), (1, 128)], "last"
    )(returned(back), gap, x, y, moments)
    (message,) = call(fold_body, [(32, 1, 128)], "fold")(exchange(message, ROW))
    out, coefficients = call(finish_body, [(32, 64), (4,)], "finish", smem=(1,))(
        exchange(message, COL), u, q_2, scalars
    )
    return out.T, coefficients


def solution(mesh):
    finer = Mesh(mesh.devices.reshape(8, 2, 4, 8), ("row_0", "row_1", "col_0", "col_1"))
    placed = (P(ROW, COL), P(ROW), P(COL), P(ROW, COL), P(COL, ROW), P(ROW, COL))
    return jax.shard_map(
        shards, mesh=finer, in_specs=placed, out_specs=(P(ROW, COL), P()), check_vma=False
    )
```

```python
import jax
import jax.numpy as jnp
from jax import lax
from jax.experimental import pallas as pl
from jax.experimental.pallas import tpu as pltpu
from jax.sharding import Mesh
from jax.sharding import PartitionSpec as P

NV = 1024
NC = 1024
COUNT = NV * NC
COL = ("col_0", "col_1")
ROW = ("row_0", "row_1")
EPS = 1e-06
SHIFT = 4.0
HIGH = lax.Precision.HIGHEST
F32 = jnp.float32


def exchange(value, axis):
    return lax.all_to_all(value, axis, 0, 0, tiled=True)


def dot(a, b, left, right):
    return lax.dot_general(
        a, b, (((left,), (right,)), ((), ())), precision=HIGH, preferred_element_type=F32
    )


def halves(value):
    upper = value.astype(jnp.bfloat16)
    return upper, (value - upper.astype(F32)).astype(jnp.bfloat16)


def dot_halves(a, b):
    (a_hi, a_lo), (b_hi, b_lo) = a, b
    return (
        jnp.dot(a_lo, b_hi, preferred_element_type=F32)
        + jnp.dot(a_hi, b_lo, preferred_element_type=F32)
        + jnp.dot(a_hi, b_hi, preferred_element_type=F32)
    )


def call(body, outs, name, smem=()):
    shapes = tuple(jax.ShapeDtypeStruct(s, F32) for s in outs)
    specs = tuple(
        pl.BlockSpec(memory_space=pltpu.SMEM if i in smem else pltpu.VMEM)
        for i in range(len(outs))
    )
    return pl.pallas_call(
        body,
        out_shape=shapes,
        out_specs=specs,
        name=name,
        compiler_params=pltpu.CompilerParams(vmem_limit_bytes=32 * 1024 * 1024),
    )


def start_body(
    block_in, panel_in, valence_in, conduction_in, packed, gap, first, second,
    block, panel, valence, conduction, arrived,
):
    moves = [
        pltpu.make_async_copy(source, target, arrived.at[i])
        for i, (source, target) in enumerate(
            [
                (block_in, block),
                (panel_in, panel),
                (valence_in, valence),
                (conduction_in, conduction),
            ]
        )
    ]
    for move in moves:
        move.start()
    for move in moves:
        move.wait()
    value = jnp.concatenate([block[0:16, :], block[16:32, :]], axis=1)
    packed[...] = value
    first[:, 0:16, :] = jnp.broadcast_to(value[None], (32, 16, 128))
    first[:, 16:48, :] = jnp.broadcast_to(panel[:, 0:128][None], (32, 32, 128))
    second[...] = jnp.broadcast_to(panel[:, 128:256][None], second.shape)
    rows = lax.broadcasted_iota(jnp.int32, (32, 32), 0)
    lanes = lax.broadcasted_iota(jnp.int32, (32, 32), 1)
    column = jnp.sum(jnp.where(rows == lanes, conduction[...], 0.0), axis=1, keepdims=True)
    half = lax.broadcasted_iota(jnp.int32, (16, 128), 1) < 64
    upper = jnp.where(half, column[0:16], column[16:32])
    gap[...] = upper - jnp.concatenate([valence[...], valence[...]], axis=1) - SHIFT


def points_of(rows, panel):
    lo = dot(rows, panel[:, 0].reshape(512, 128), 0, 0)
    hi = dot(rows, panel[:, 1].reshape(512, 128), 0, 0)
    return lo[0:64] + hi[64:128]


def first_points_body(first, panel, out):
    out[...] = points_of(first[:, 0:16, :].reshape(512, 128), panel)


def second_points_body(first, y_rows, panel, out):
    x = first[:, 0:16, :].reshape(512, 128)
    y = y_rows[...].reshape(512, 128)
    sums = [jnp.sum(a * b, axis=0, keepdims=True) for a, b in ((x, x), (x, y), (y, y))]
    message = jnp.concatenate([points_of(y, panel), *sums, jnp.zeros((5, 128), F32)], axis=0)
    out[...] = jnp.broadcast_to(message[None], out.shape)


def weigh(image, first, second, screened, out):
    panel = jnp.concatenate(
        [first[:, 16:48, :].reshape(1024, 128), second[...].reshape(1024, 128)], axis=1
    )
    panel = halves(panel)
    points = dot_halves(halves(image.T), panel).T
    back = dot_halves(panel, halves(points * screened[...])).reshape(8, 2, 64, 128)
    out[0] = back[:, 0]
    out[1] = back[:, 1]


def first_weigh_body(image, first, second, screened, out):
    weigh(image[...], first, second, screened, out)


def second_weigh_body(arrived, first, second, screened, out, moments):
    image = jnp.stack([arrived[0, :, 0:64, :], arrived[1, :, 0:64, :]], axis=1)
    weigh(image.reshape(1024, 128), first, second, screened, out)
    moments[...] = jnp.sum(arrived[0, :, 64:72, :] + arrived[1, :, 64:72, :], axis=0)


def pair_body(parts, out):
    out[...] = parts[0] + parts[1]


def conduct_body(parts, panel, out):
    back = jnp.sum(parts[...], axis=0)
    zero = jnp.zeros_like(back)
    lo = dot(panel[:, 0].reshape(512, 128), jnp.concatenate([back, zero], axis=0), 1, 1)
    hi = dot(panel[:, 1].reshape(512, 128), jnp.concatenate([zero, back], axis=0), 1, 1)
    out[...] = (lo + hi).reshape(32, 16, 128)


def update_body(parts, gap, x, packed, spread):
    value = gap[...] * x[...] - jnp.sum(parts[...], axis=0)
    packed[...] = value
    spread[...] = jnp.broadcast_to(value[None], spread.shape)


def total(value):
    return jnp.sum(jnp.sum(value, axis=0, keepdims=True), axis=1, keepdims=True)


def last_body(parts, gap, x, y, moments, u_out, q_out, message, scalars):
    norm = total(moments[0:1, :]) / COUNT
    inverse = 1.0 / jnp.sqrt(norm + EPS)
    first_norm = norm * inverse * inverse
    first_cross = total(moments[1:2, :]) / COUNT * inverse * inverse
    alpha = first_cross + SHIFT * first_norm
    rest = alpha - SHIFT
    beta = jnp.sqrt(
        total(moments[2:3, :]) / COUNT * inverse * inverse
        - 2.0 * rest * first_cross
        + rest * rest * first_norm
        + EPS
    )
    z = gap[...] * y[...] - jnp.sum(parts[...], axis=0)
    q_1 = x[...] * inverse
    scale = inverse / beta
    q_2 = (y[...] - rest * x[...]) * scale
    u = (z - rest * y[...]) * scale - beta * q_1
    u_out[...] = u
    q_out[...] = q_2
    lane = lax.broadcasted_iota(jnp.int32, (1, 128), 1)
    row = jnp.where(lane < 32, total(u * u), total(u * q_2))
    row = jnp.where(lane < 64, row, jnp.where(lane < 96, total(q_2 * q_2), total(q_1 * q_2)))
    message[...] = jnp.broadcast_to(row[None], message.shape)
    scalars[...] = jnp.where(lane < 64, alpha, beta)


def fold_body(parts, message):
    row = jnp.sum(parts[...], axis=0)
    message[...] = jnp.broadcast_to(row[None], message.shape)


def finish_body(parts, u, q_2, scalars, out, coefficients):
    row = jnp.sum(parts[...], axis=0) / COUNT
    uu, uq, qq, oq = row[:, 0:1], row[:, 32:33], row[:, 64:65], row[:, 96:97]
    beta_1 = scalars[:, 64:65]
    alpha = uq + beta_1 * oq + SHIFT * qq
    rest = alpha - SHIFT
    beta = jnp.sqrt(uu - 2.0 * rest * uq + rest * rest * qq + EPS)
    value = (u[...] - rest * q_2[...]) / beta
    out[0:16, :] = value[:, 0:64]
    out[16:32, :] = value[:, 64:128]
    coefficients[0] = scalars[0, 0]
    coefficients[1] = scalars[0, 64]
    coefficients[2] = alpha[0, 0]
    coefficients[3] = beta[0, 0]


def shards(excitons, valence_energy, conduction_energy, psi_valence, psi_conduction, screened):
    x, gap, first, second = pl.pallas_call(
        start_body,
        out_shape=tuple(
            jax.ShapeDtypeStruct(shape, F32)
            for shape in [(16, 128), (16, 128), (32, 48, 128), (32, 32, 128)]
        ),
        in_specs=[pl.BlockSpec(memory_space=pltpu.HBM)] * 4,
        out_specs=(pl.BlockSpec(memory_space=pltpu.VMEM),) * 4,
        scratch_shapes=[
            pltpu.VMEM((32, 64), F32),
            pltpu.VMEM((32, 256), F32),
            pltpu.VMEM((1, 64), F32),
            pltpu.VMEM((1, 32), F32),
            pltpu.SemaphoreType.DMA((4,)),
        ],
        name="start",
        compiler_params=pltpu.CompilerParams(vmem_limit_bytes=32 * 1024 * 1024),
    )(
        *(
            pltpu.with_memory_space_constraint(value, pltpu.HBM)
            for value in (
                excitons.T,
                psi_valence.T,
                valence_energy[None],
                conduction_energy[None],
            )
        )
    )
    first = exchange(first, COL)
    panel_conduction = lax.all_gather(psi_conduction.T, ROW, axis=0, tiled=True)
    panel_conduction = panel_conduction.reshape(32, 2, 16, 128)

    def returned(back):
        (back,) = call(pair_body, [(8, 64, 128)], "pair")(exchange(back, "row_1"))
        back = exchange(back, "row_0")
        (kernel,) = call(conduct_body, [(32, 16, 128)], "conduct")(back, panel_conduction)
        return exchange(kernel, COL)

    (image,) = call(first_points_body, [(64, 128)], "points_one")(first, panel_conduction)
    image, second = lax.optimization_barrier((image, second))
    second = exchange(second, COL)
    image = lax.all_gather(image, ROW, axis=0, tiled=True)
    (back,) = call(first_weigh_body, [(2, 8, 64, 128)], "weigh_one")(image, first, second, screened)
    y, spread = call(update_body, [(16, 128), (32, 16, 128)], "update")(returned(back), gap, x)

    y_rows = exchange(spread, COL)
    (image,) = call(second_points_body, [(8, 72, 128)], "points_two")(
        first, y_rows, panel_conduction
    )
    image = lax.all_gather(exchange(image, "row_0"), "row_1", axis=0)
    back, moments = call(second_weigh_body, [(2, 8, 64, 128), (8, 128)], "weigh_two")(
        image, first, second, screened
    )
    u, q_2, message, scalars = call(
        last_body, [(16, 128), (16, 128), (64, 1, 128), (1, 128)], "last"
    )(returned(back), gap, x, y, moments)
    (message,) = call(fold_body, [(8, 1, 128)], "fold")(exchange(message, (*ROW, "col_0")))
    out, coefficients = call(finish_body, [(32, 64), (4,)], "finish", smem=(1,))(
        exchange(message, "col_1"), u, q_2, scalars
    )
    return out.T, coefficients


def solution(mesh):
    finer = Mesh(mesh.devices.reshape(8, 2, 4, 8), ("row_0", "row_1", "col_0", "col_1"))
    placed = (P(ROW, COL), P(ROW), P(COL), P(ROW, COL), P(COL, ROW), P(ROW, COL))
    return jax.shard_map(
        shards, mesh=finer, in_specs=placed, out_specs=(P(ROW, COL), P()), check_vma=False
    )
```

```python
import jax
import jax.numpy as jnp
from jax import lax
from jax.experimental import pallas as pl
from jax.experimental.pallas import tpu as pltpu
from jax.sharding import Mesh
from jax.sharding import PartitionSpec as P

NV = 1024
NC = 1024
COUNT = NV * NC
COL = ("col_0", "col_1")
ROW = ("row_0", "row_1")
EPS = 1e-06
SHIFT = 4.0
HIGH = lax.Precision.HIGHEST
F32 = jnp.float32


def exchange(value, axis):
    return lax.all_to_all(value, axis, 0, 0, tiled=True)


def dot(a, b, left, right):
    return lax.dot_general(
        a, b, (((left,), (right,)), ((), ())), precision=HIGH, preferred_element_type=F32
    )


def halves(value):
    upper = value.astype(jnp.bfloat16)
    return upper, (value - upper.astype(F32)).astype(jnp.bfloat16)


def dot_halves(a, b):
    (a_hi, a_lo), (b_hi, b_lo) = a, b
    return (
        jnp.dot(a_lo, b_hi, preferred_element_type=F32)
        + jnp.dot(a_hi, b_lo, preferred_element_type=F32)
        + jnp.dot(a_hi, b_hi, preferred_element_type=F32)
    )


def call(body, outs, name, smem=()):
    shapes = tuple(jax.ShapeDtypeStruct(s, F32) for s in outs)
    specs = tuple(
        pl.BlockSpec(memory_space=pltpu.SMEM if i in smem else pltpu.VMEM)
        for i in range(len(outs))
    )
    return pl.pallas_call(
        body,
        out_shape=shapes,
        out_specs=specs,
        name=name,
        compiler_params=pltpu.CompilerParams(vmem_limit_bytes=32 * 1024 * 1024),
    )


def mine(zero, one):
    return jnp.where(lax.axis_index("row_1") == 0, zero, one)


def spread_half(out, at, half):
    out[:, at : at + 16, :] = jnp.broadcast_to(half[:, 0:128][None], (32, 16, 128))
    out[:, at + 16 : at + 32, :] = jnp.broadcast_to(half[:, 128:256][None], (32, 16, 128))


def start_body(
    block_in, panel_in, valence_in, conduction_in, packed, gap, first,
    block, panel, valence, conduction, arrived,
):
    moves = [
        pltpu.make_async_copy(source, target, arrived.at[i])
        for i, (source, target) in enumerate(
            [
                (block_in, block),
                (panel_in, panel),
                (valence_in, valence),
                (conduction_in, conduction),
            ]
        )
    ]
    for move in moves:
        move.start()
    for move in moves:
        move.wait()
    value = jnp.concatenate([block[0:16, :], block[16:32, :]], axis=1)
    packed[...] = value
    first[:, 0:16, :] = jnp.broadcast_to(value[None], (32, 16, 128))
    spread_half(first, 16, mine(panel[0:16, :], panel[16:32, :]))
    rows = lax.broadcasted_iota(jnp.int32, (32, 32), 0)
    lanes = lax.broadcasted_iota(jnp.int32, (32, 32), 1)
    column = jnp.sum(jnp.where(rows == lanes, conduction[...], 0.0), axis=1, keepdims=True)
    half = lax.broadcasted_iota(jnp.int32, (16, 128), 1) < 64
    upper = jnp.where(half, column[0:16], column[16:32])
    gap[...] = upper - jnp.concatenate([valence[...], valence[...]], axis=1) - SHIFT


def points_of(rows, panel):
    lo = dot(rows, panel[:, 0].reshape(512, 128), 0, 0)
    hi = dot(rows, panel[:, 1].reshape(512, 128), 0, 0)
    return lo[0:64] + hi[64:128]


def first_points_body(first, panel, blocks, out, second):
    out[...] = points_of(first[:, 0:16, :].reshape(512, 128), panel)
    spread_half(second, 0, mine(blocks[1, 0:16, :], blocks[0, 16:32, :]))


def second_points_body(first, y_rows, panel, out):
    x = first[:, 0:16, :].reshape(512, 128)
    y = y_rows[...].reshape(512, 128)
    sums = [jnp.sum(a * b, axis=0, keepdims=True) for a, b in ((x, x), (x, y), (y, y))]
    sums.append(jnp.zeros((5, 128), F32))
    image = points_of(y, panel)
    for core in range(2):
        at = 16 * core
        message = [image[at : at + 16], image[at + 32 : at + 48], *sums]
        message = jnp.concatenate(message, axis=0)
        out[:, core] = jnp.broadcast_to(message[None], (8, 40, 128))


def shared_panel(first, second):
    parts = [first[:, 16:32, :], first[:, 32:48, :], second[:, 0:16, :], second[:, 16:32, :]]
    return halves(jnp.concatenate([part.reshape(512, 128) for part in parts], axis=1))


def partial_points(image, first, second, out):
    points = dot_halves(halves(image.T), shared_panel(first, second)).T
    out[0] = mine(points[0:256], points[256:512])
    out[1] = mine(points[256:512], points[0:256])


def first_partial_body(image, first, second, out):
    image = mine(image[:, 0], image[:, 1]).reshape(512, 128)
    partial_points(image, first, second, out)


def second_partial_body(arrived, first, second, out, moments):
    partial_points(arrived[:, 0:32, :].reshape(512, 128), first, second, out)
    moments[...] = jnp.sum(arrived[:, 32:40, :], axis=0)


def weigh_body(partials, screened, first, second, out):
    zero = (partials[0, 0] + partials[1, 0]) * screened[0]
    one = (partials[0, 1] + partials[1, 1]) * screened[1]
    weighted = jnp.concatenate([mine(zero, one), mine(one, zero)], axis=0)
    back = dot_halves(shared_panel(first, second), halves(weighted))
    out[...] = back.reshape(16, 32, 128)


def conduct_body(parts, panel, out):
    sums = jnp.sum(parts[...], axis=0)
    back = jnp.stack([sums[0].reshape(2, 16, 128), sums[1].reshape(2, 16, 128)], axis=1)
    back = back.reshape(64, 128)
    zero = jnp.zeros_like(back)
    lo = dot(panel[:, 0].reshape(512, 128), jnp.concatenate([back, zero], axis=0), 1, 1)
    hi = dot(panel[:, 1].reshape(512, 128), jnp.concatenate([zero, back], axis=0), 1, 1)
    out[...] = (lo + hi).reshape(32, 16, 128)


def update_body(parts, gap, x, packed, spread):
    value = gap[...] * x[...] - jnp.sum(parts[...], axis=0)
    packed[...] = value
    spread[...] = jnp.broadcast_to(value[None], spread.shape)


def total(value):
    return jnp.sum(jnp.sum(value, axis=0, keepdims=True), axis=1, keepdims=True)


def last_body(parts, gap, x, y, moments, u_out, q_out, message, scalars):
    norm = total(moments[0:1, :]) / COUNT
    inverse = 1.0 / jnp.sqrt(norm + EPS)
    first_norm = norm * inverse * inverse
    first_cross = total(moments[1:2, :]) / COUNT * inverse * inverse
    alpha = first_cross + SHIFT * first_norm
    rest = alpha - SHIFT
    beta = jnp.sqrt(
        total(moments[2:3, :]) / COUNT * inverse * inverse
        - 2.0 * rest * first_cross
        + rest * rest * first_norm
        + EPS
    )
    z = gap[...] * y[...] - jnp.sum(parts[...], axis=0)
    q_1 = x[...] * inverse
    scale = inverse / beta
    q_2 = (y[...] - rest * x[...]) * scale
    u = (z - rest * y[...]) * scale - beta * q_1
    u_out[...] = u
    q_out[...] = q_2
    lane = lax.broadcasted_iota(jnp.int32, (1, 128), 1)
    row = jnp.where(lane < 32, total(u * u), total(u * q_2))
    row = jnp.where(lane < 64, row, jnp.where(lane < 96, total(q_2 * q_2), total(q_1 * q_2)))
    message[...] = jnp.broadcast_to(row[None], message.shape)
    scalars[...] = jnp.where(lane < 64, alpha, beta)


def fold_body(parts, message):
    row = jnp.sum(parts[...], axis=0)
    message[...] = jnp.broadcast_to(row[None], message.shape)


def finish_body(parts, u, q_2, scalars, out, coefficients):
    row = jnp.sum(parts[...], axis=0) / COUNT
    uu, uq, qq, oq = row[:, 0:1], row[:, 32:33], row[:, 64:65], row[:, 96:97]
    beta_1 = scalars[:, 64:65]
    alpha = uq + beta_1 * oq + SHIFT * qq
    rest = alpha - SHIFT
    beta = jnp.sqrt(uu - 2.0 * rest * uq + rest * rest * qq + EPS)
    value = (u[...] - rest * q_2[...]) / beta
    out[0:16, :] = value[:, 0:64]
    out[16:32, :] = value[:, 64:128]
    coefficients[0] = scalars[0, 0]
    coefficients[1] = scalars[0, 64]
    coefficients[2] = alpha[0, 0]
    coefficients[3] = beta[0, 0]


def shards(excitons, valence_energy, conduction_energy, psi_valence, psi_conduction, screened):
    x, gap, first = pl.pallas_call(
        start_body,
        out_shape=tuple(
            jax.ShapeDtypeStruct(shape, F32) for shape in [(16, 128), (16, 128), (32, 48, 128)]
        ),
        in_specs=[pl.BlockSpec(memory_space=pltpu.HBM)] * 4,
        out_specs=(pl.BlockSpec(memory_space=pltpu.VMEM),) * 3,
        scratch_shapes=[
            pltpu.VMEM((32, 64), F32),
            pltpu.VMEM((32, 256), F32),
            pltpu.VMEM((1, 64), F32),
            pltpu.VMEM((1, 32), F32),
            pltpu.SemaphoreType.DMA((4,)),
        ],
        name="start",
        compiler_params=pltpu.CompilerParams(vmem_limit_bytes=32 * 1024 * 1024),
    )(
        *(
            pltpu.with_memory_space_constraint(value, pltpu.HBM)
            for value in (
                excitons.T,
                psi_valence.T,
                valence_energy[None],
                conduction_energy[None],
            )
        )
    )
    first = exchange(first, COL)
    panel_conduction = lax.all_gather(psi_conduction.T, ROW, axis=0, tiled=True)
    panel_conduction = panel_conduction.reshape(32, 2, 16, 128)

    blocks = lax.all_gather(psi_valence.T, "row_1", axis=0)
    pair_screened = lax.all_gather(screened, "row_1", axis=0)
    blocks, pair_screened = lax.optimization_barrier((blocks, pair_screened))

    def returned(partial):
        partials = lax.all_gather(partial, "row_1", axis=0)
        (back,) = call(weigh_body, [(16, 32, 128)], "weigh")(
            partials, pair_screened, first, second
        )
        back = exchange(back, ROW).reshape(8, 2, 32, 128)
        (kernel,) = call(conduct_body, [(32, 16, 128)], "conduct")(back, panel_conduction)
        return exchange(kernel, COL)

    image, second = call(first_points_body, [(64, 128), (32, 32, 128)], "points_one")(
        first, panel_conduction, blocks
    )
    second = exchange(second, COL)
    image = lax.all_gather(image, ROW, axis=0, tiled=True).reshape(32, 2, 16, 128)
    (partial,) = call(first_partial_body, [(2, 256, 128)], "partial_one")(image, first, second)
    y, spread = call(update_body, [(16, 128), (32, 16, 128)], "update")(returned(partial), gap, x)

    y_rows = exchange(spread, COL)
    (image,) = call(second_points_body, [(8, 2, 40, 128)], "points_two")(
        first, y_rows, panel_conduction
    )
    image = exchange(image.reshape(16, 40, 128), ROW)
    partial, moments = call(second_partial_body, [(2, 256, 128), (8, 128)], "partial_two")(
        image, first, second
    )
    u, q_2, message, scalars = call(
        last_body, [(16, 128), (16, 128), (64, 1, 128), (1, 128)], "last"
    )(returned(partial), gap, x, y, moments)
    (message,) = call(fold_body, [(8, 1, 128)], "fold")(exchange(message, (*ROW, "col_0")))
    out, coefficients = call(finish_body, [(32, 64), (4,)], "finish", smem=(1,))(
        exchange(message, "col_1"), u, q_2, scalars
    )
    return out.T, coefficients


def solution(mesh):
    finer = Mesh(mesh.devices.reshape(8, 2, 4, 8), ("row_0", "row_1", "col_0", "col_1"))
    placed = (P(ROW, COL), P(ROW), P(COL), P(ROW, COL), P(COL, ROW), P(ROW, COL))
    return jax.shard_map(
        shards, mesh=finer, in_specs=placed, out_specs=(P(ROW, COL), P()), check_vma=False
    )
```

```python
import jax
import jax.numpy as jnp
from jax import lax
from jax.experimental import pallas as pl
from jax.experimental.pallas import tpu as pltpu
from jax.sharding import Mesh
from jax.sharding import PartitionSpec as P

NV = 1024
NC = 1024
COUNT = NV * NC
COL = ("col_0", "col_1")
ROW = ("row_0", "row_1")
EPS = 1e-06
SHIFT = 4.0
F32 = jnp.float32


def exchange(value, axis):
    return lax.all_to_all(value, axis, 0, 0, tiled=True)


def halves(value):
    upper = value.astype(jnp.bfloat16)
    return upper, (value - upper.astype(F32)).astype(jnp.bfloat16)


def dot_halves(a, b):
    (a_hi, a_lo), (b_hi, b_lo) = a, b
    return (
        jnp.dot(a_lo, b_hi, preferred_element_type=F32)
        + jnp.dot(a_hi, b_lo, preferred_element_type=F32)
        + jnp.dot(a_hi, b_hi, preferred_element_type=F32)
    )


def call(body, outs, name, smem=()):
    shapes = tuple(jax.ShapeDtypeStruct(s, F32) for s in outs)
    specs = tuple(
        pl.BlockSpec(memory_space=pltpu.SMEM if i in smem else pltpu.VMEM)
        for i in range(len(outs))
    )
    return pl.pallas_call(
        body,
        out_shape=shapes,
        out_specs=specs,
        name=name,
        compiler_params=pltpu.CompilerParams(vmem_limit_bytes=32 * 1024 * 1024),
    )


def start_body(
    block_in, panel_in, valence_in, conduction_in, packed, gap, first,
    block, panel, valence, conduction, arrived,
):
    moves = [
        pltpu.make_async_copy(source, target, arrived.at[i])
        for i, (source, target) in enumerate(
            [
                (block_in, block),
                (panel_in, panel),
                (valence_in, valence),
                (conduction_in, conduction),
            ]
        )
    ]
    for move in moves:
        move.start()
    for move in moves:
        move.wait()
    value = jnp.concatenate([block[0:16, :], block[16:32, :]], axis=1)
    packed[...] = value
    first[:, 0:16, :] = jnp.broadcast_to(value[None], (32, 16, 128))
    first[:, 16:48, :] = jnp.broadcast_to(panel[:, 0:128][None], (32, 32, 128))
    rows = lax.broadcasted_iota(jnp.int32, (32, 32), 0)
    lanes = lax.broadcasted_iota(jnp.int32, (32, 32), 1)
    column = jnp.sum(jnp.where(rows == lanes, conduction[...], 0.0), axis=1, keepdims=True)
    half = lax.broadcasted_iota(jnp.int32, (16, 128), 1) < 64
    upper = jnp.where(half, column[0:16], column[16:32])
    gap[...] = upper - jnp.concatenate([valence[...], valence[...]], axis=1) - SHIFT


def spread_body(panel, second):
    second[...] = jnp.broadcast_to(panel[:, 128:256][None], second.shape)


def points_of(rows, panel):
    rows = halves(rows.T)
    lo = dot_halves(rows, halves(panel[:, 0].reshape(512, 128)))
    hi = dot_halves(rows, halves(panel[:, 1].reshape(512, 128)))
    return lo[0:64] + hi[64:128]


def first_points_body(first, panel, out):
    out[...] = points_of(first[:, 0:16, :].reshape(512, 128), panel)


def second_points_body(first, y_rows, panel, out):
    x = first[:, 0:16, :].reshape(512, 128)
    y = y_rows[...].reshape(512, 128)
    sums = [jnp.sum(a * b, axis=0, keepdims=True) for a, b in ((x, x), (x, y), (y, y))]
    message = jnp.concatenate([points_of(y, panel), *sums, jnp.zeros((5, 128), F32)], axis=0)
    out[...] = jnp.broadcast_to(message[None], out.shape)


def weigh(image, first, second, screened, out):
    panel = jnp.concatenate(
        [first[:, 16:48, :].reshape(1024, 128), second[...].reshape(1024, 128)], axis=1
    )
    panel = halves(panel)
    points = dot_halves(halves(image.T), panel).T
    back = dot_halves(panel, halves(points * screened[...])).reshape(8, 2, 64, 128)
    out[0] = back[:, 0]
    out[1] = back[:, 1]


def first_weigh_body(image, first, second, screened, out):
    weigh(image[...], first, second, screened, out)


def second_weigh_body(arrived, first, second, screened, out, moments):
    image = jnp.stack([arrived[0, :, 0:64, :], arrived[1, :, 0:64, :]], axis=1)
    weigh(image.reshape(1024, 128), first, second, screened, out)
    moments[...] = jnp.sum(arrived[0, :, 64:72, :] + arrived[1, :, 64:72, :], axis=0)


def pair_body(parts, out):
    out[...] = parts[0] + parts[1]


def conduct_body(parts, panel, out):
    back = jnp.sum(parts[...], axis=0).T
    zero = jnp.zeros_like(back)
    lo = dot_halves(
        halves(panel[:, 0].reshape(512, 128)), halves(jnp.concatenate([back, zero], axis=1))
    )
    hi = dot_halves(
        halves(panel[:, 1].reshape(512, 128)), halves(jnp.concatenate([zero, back], axis=1))
    )
    out[...] = (lo + hi).reshape(32, 16, 128)


def update_body(parts, gap, x, packed, spread):
    value = gap[...] * x[...] - jnp.sum(parts[...], axis=0)
    packed[...] = value
    spread[...] = jnp.broadcast_to(value[None], spread.shape)


def total(value):
    return jnp.sum(jnp.sum(value, axis=0, keepdims=True), axis=1, keepdims=True)


def last_body(parts, gap, x, y, moments, u_out, q_out, message, scalars):
    norm = total(moments[0:1, :]) / COUNT
    inverse = 1.0 / jnp.sqrt(norm + EPS)
    first_norm = norm * inverse * inverse
    first_cross = total(moments[1:2, :]) / COUNT * inverse * inverse
    alpha = first_cross + SHIFT * first_norm
    rest = alpha - SHIFT
    beta = jnp.sqrt(
        total(moments[2:3, :]) / COUNT * inverse * inverse
        - 2.0 * rest * first_cross
        + rest * rest * first_norm
        + EPS
    )
    z = gap[...] * y[...] - jnp.sum(parts[...], axis=0)
    q_1 = x[...] * inverse
    scale = inverse / beta
    q_2 = (y[...] - rest * x[...]) * scale
    u = (z - rest * y[...]) * scale - beta * q_1
    u_out[...] = u
    q_out[...] = q_2
    lane = lax.broadcasted_iota(jnp.int32, (1, 128), 1)
    row = jnp.where(lane < 32, total(u * u), total(u * q_2))
    row = jnp.where(lane < 64, row, jnp.where(lane < 96, total(q_2 * q_2), total(q_1 * q_2)))
    message[...] = jnp.broadcast_to(row[None], message.shape)
    scalars[...] = jnp.where(lane < 64, alpha, beta)


def fold_body(parts, message):
    row = jnp.sum(parts[...], axis=0)
    message[...] = jnp.broadcast_to(row[None], message.shape)


def finish_body(parts, u, q_2, scalars, out, coefficients):
    row = jnp.sum(parts[...], axis=0) / COUNT
    uu, uq, qq, oq = row[:, 0:1], row[:, 32:33], row[:, 64:65], row[:, 96:97]
    beta_1 = scalars[:, 64:65]
    alpha = uq + beta_1 * oq + SHIFT * qq
    rest = alpha - SHIFT
    beta = jnp.sqrt(uu - 2.0 * rest * uq + rest * rest * qq + EPS)
    value = (u[...] - rest * q_2[...]) / beta
    out[0:16, :] = value[:, 0:64]
    out[16:32, :] = value[:, 64:128]
    coefficients[0] = scalars[0, 0]
    coefficients[1] = scalars[0, 64]
    coefficients[2] = alpha[0, 0]
    coefficients[3] = beta[0, 0]


def shards(excitons, valence_energy, conduction_energy, psi_valence, psi_conduction, screened):
    x, gap, first = pl.pallas_call(
        start_body,
        out_shape=tuple(
            jax.ShapeDtypeStruct(shape, F32) for shape in [(16, 128), (16, 128), (32, 48, 128)]
        ),
        in_specs=[pl.BlockSpec(memory_space=pltpu.HBM)] * 4,
        out_specs=(pl.BlockSpec(memory_space=pltpu.VMEM),) * 3,
        scratch_shapes=[
            pltpu.VMEM((32, 64), F32),
            pltpu.VMEM((32, 256), F32),
            pltpu.VMEM((1, 64), F32),
            pltpu.VMEM((1, 32), F32),
            pltpu.SemaphoreType.DMA((4,)),
        ],
        name="start",
        compiler_params=pltpu.CompilerParams(vmem_limit_bytes=32 * 1024 * 1024),
    )(
        *(
            pltpu.with_memory_space_constraint(value, pltpu.HBM)
            for value in (
                excitons.T,
                psi_valence.T,
                valence_energy[None],
                conduction_energy[None],
            )
        )
    )
    first = exchange(first, COL)
    panel_conduction = lax.all_gather(psi_conduction.T, ROW, axis=0, tiled=True)
    panel_conduction = panel_conduction.reshape(32, 2, 16, 128)
    (second,) = call(spread_body, [(32, 32, 128)], "spread")(psi_valence.T)
    panel_conduction, second = lax.optimization_barrier((panel_conduction, second))

    def returned(back):
        (back,) = call(pair_body, [(8, 64, 128)], "pair")(exchange(back, "row_1"))
        back = exchange(back, "row_0")
        (kernel,) = call(conduct_body, [(32, 16, 128)], "conduct")(back, panel_conduction)
        return exchange(kernel, COL)

    (image,) = call(first_points_body, [(64, 128)], "points_one")(first, panel_conduction)
    image, second = lax.optimization_barrier((image, second))
    second = exchange(second, COL)
    image = lax.all_gather(image, ROW, axis=0, tiled=True)
    (back,) = call(first_weigh_body, [(2, 8, 64, 128)], "weigh_one")(image, first, second, screened)
    y, spread = call(update_body, [(16, 128), (32, 16, 128)], "update")(returned(back), gap, x)

    y_rows = exchange(spread, COL)
    (image,) = call(second_points_body, [(8, 72, 128)], "points_two")(
        first, y_rows, panel_conduction
    )
    image = lax.all_gather(exchange(image, "row_0"), "row_1", axis=0)
    back, moments = call(second_weigh_body, [(2, 8, 64, 128), (8, 128)], "weigh_two")(
        image, first, second, screened
    )
    u, q_2, message, scalars = call(
        last_body, [(16, 128), (16, 128), (64, 1, 128), (1, 128)], "last"
    )(returned(back), gap, x, y, moments)
    (message,) = call(fold_body, [(8, 1, 128)], "fold")(exchange(message, (*ROW, "col_0")))
    out, coefficients = call(finish_body, [(32, 64), (4,)], "finish", smem=(1,))(
        exchange(message, "col_1"), u, q_2, scalars
    )
    return out.T, coefficients


def solution(mesh):
    finer = Mesh(mesh.devices.reshape(8, 2, 4, 8), ("row_0", "row_1", "col_0", "col_1"))
    placed = (P(ROW, COL), P(ROW), P(COL), P(ROW, COL), P(COL, ROW), P(ROW, COL))
    return jax.shard_map(
        shards, mesh=finer, in_specs=placed, out_specs=(P(ROW, COL), P()), check_vma=False
    )
```

```python
import jax
import jax.numpy as jnp
from jax import lax
from jax.experimental import pallas as pl
from jax.experimental.pallas import tpu as pltpu
from jax.sharding import Mesh
from jax.sharding import PartitionSpec as P

NV = 1024
NC = 1024
COUNT = NV * NC
COL = ("col_0", "col_1")
ROW = ("row_0", "row_1")
EPS = 1e-06
SHIFT = 4.0
F32 = jnp.float32


def exchange(value, axis):
    return lax.all_to_all(value, axis, 0, 0, tiled=True)


def halves(value):
    upper = value.astype(jnp.bfloat16)
    return upper, (value - upper.astype(F32)).astype(jnp.bfloat16)


def dot_halves(a, b):
    (a_hi, a_lo), (b_hi, b_lo) = a, b
    return (
        jnp.dot(a_lo, b_hi, preferred_element_type=F32)
        + jnp.dot(a_hi, b_lo, preferred_element_type=F32)
        + jnp.dot(a_hi, b_hi, preferred_element_type=F32)
    )


def call(body, outs, name, smem=()):
    shapes = tuple(jax.ShapeDtypeStruct(s, F32) for s in outs)
    specs = tuple(
        pl.BlockSpec(memory_space=pltpu.SMEM if i in smem else pltpu.VMEM)
        for i in range(len(outs))
    )
    return pl.pallas_call(
        body,
        out_shape=shapes,
        out_specs=specs,
        name=name,
        compiler_params=pltpu.CompilerParams(vmem_limit_bytes=32 * 1024 * 1024),
    )


def mine(zero, one):
    return jnp.where(lax.axis_index("row_1") == 0, zero, one)


def spread_half(out, at, low, high):
    out[:, at : at + 16, :] = jnp.broadcast_to(low[None], (32, 16, 128))
    out[:, at + 16 : at + 32, :] = jnp.broadcast_to(high[None], (32, 16, 128))


def start_body(
    block_in, panel_in, valence_in, conduction_in, screened_in, packed, gap, first, pair,
    block, panel, valence, conduction, arrived,
):
    moves = [
        pltpu.make_async_copy(source, target, arrived.at[i])
        for i, (source, target) in enumerate(
            [
                (block_in, block),
                (panel_in, panel),
                (valence_in, valence),
                (conduction_in, conduction),
                (screened_in, pair.at[64:320]),
            ]
        )
    ]
    for move in moves:
        move.start()
    for move in moves[:4]:
        move.wait()
    value = jnp.concatenate([block[0:16, :], block[16:32, :]], axis=1)
    packed[...] = value
    first[:, 0:16, :] = jnp.broadcast_to(value[None], (32, 16, 128))
    half = mine(panel[0:16, :], panel[16:32, :])
    spread_half(first, 16, half[:, 0:128], half[:, 128:256])
    rows = lax.broadcasted_iota(jnp.int32, (32, 32), 0)
    lanes = lax.broadcasted_iota(jnp.int32, (32, 32), 1)
    column = jnp.sum(jnp.where(rows == lanes, conduction[...], 0.0), axis=1, keepdims=True)
    half = lax.broadcasted_iota(jnp.int32, (16, 128), 1) < 64
    upper = jnp.where(half, column[0:16], column[16:32])
    gap[...] = upper - jnp.concatenate([valence[...], valence[...]], axis=1) - SHIFT
    pair[0:32, :] = panel[:, 0:128]
    pair[32:64, :] = panel[:, 128:256]
    moves[4].wait()


def points_of(rows, panel):
    rows = halves(rows.T)
    lo = dot_halves(rows, halves(panel[:, 0].reshape(512, 128)))
    hi = dot_halves(rows, halves(panel[:, 1].reshape(512, 128)))
    return lo[0:64] + hi[64:128]


def spread_body(pair, second):
    low = mine(pair[1, 0:16, :], pair[0, 16:32, :])
    spread_half(second, 0, low, mine(pair[1, 32:48, :], pair[0, 48:64, :]))


def first_points_body(first, panel, out):
    out[...] = points_of(first[:, 0:16, :].reshape(512, 128), panel)


def second_points_body(first, y_rows, panel, out):
    x = first[:, 0:16, :].reshape(512, 128)
    y = y_rows[...].reshape(512, 128)
    sums = [jnp.sum(a * b, axis=0, keepdims=True) for a, b in ((x, x), (x, y), (y, y))]
    sums.append(jnp.zeros((5, 128), F32))
    image = points_of(y, panel)
    for core in range(2):
        at = 16 * core
        message = [image[at : at + 16], image[at + 32 : at + 48], *sums]
        message = jnp.concatenate(message, axis=0)
        out[:, core] = jnp.broadcast_to(message[None], (8, 40, 128))


def shared_panel(first, second):
    parts = [first[:, 16:32, :], first[:, 32:48, :], second[:, 0:16, :], second[:, 16:32, :]]
    return halves(jnp.concatenate([part.reshape(512, 128) for part in parts], axis=1))


def partial_points(image, first, second, out):
    points = dot_halves(halves(image.T), shared_panel(first, second)).T
    out[0] = mine(points[0:256], points[256:512])
    out[1] = mine(points[256:512], points[0:256])


def first_partial_body(image, first, second, out):
    image = mine(image[:, 0], image[:, 1]).reshape(512, 128)
    partial_points(image, first, second, out)


def second_partial_body(arrived, first, second, out, moments):
    partial_points(arrived[:, 0:32, :].reshape(512, 128), first, second, out)
    moments[...] = jnp.sum(arrived[:, 32:40, :], axis=0)


def weigh_body(partials, pair, first, second, out):
    zero = (partials[0, 0] + partials[1, 0]) * pair[0, 64:320, :]
    one = (partials[0, 1] + partials[1, 1]) * pair[1, 64:320, :]
    weighted = jnp.concatenate([mine(zero, one), mine(one, zero)], axis=0)
    back = dot_halves(shared_panel(first, second), halves(weighted))
    out[...] = back.reshape(16, 32, 128)


def conduct_body(parts, panel, out):
    sums = jnp.sum(parts[...], axis=0)
    back = jnp.stack([sums[0].reshape(2, 16, 128), sums[1].reshape(2, 16, 128)], axis=1)
    back = back.reshape(64, 128).T
    zero = jnp.zeros_like(back)
    lo = dot_halves(
        halves(panel[:, 0].reshape(512, 128)), halves(jnp.concatenate([back, zero], axis=1))
    )
    hi = dot_halves(
        halves(panel[:, 1].reshape(512, 128)), halves(jnp.concatenate([zero, back], axis=1))
    )
    out[...] = (lo + hi).reshape(32, 16, 128)


def update_body(parts, gap, x, packed, spread):
    value = gap[...] * x[...] - jnp.sum(parts[...], axis=0)
    packed[...] = value
    spread[...] = jnp.broadcast_to(value[None], spread.shape)


def total(value):
    return jnp.sum(jnp.sum(value, axis=0, keepdims=True), axis=1, keepdims=True)


def last_body(parts, gap, x, y, moments, u_out, q_out, message, scalars):
    norm = total(moments[0:1, :]) / COUNT
    inverse = 1.0 / jnp.sqrt(norm + EPS)
    first_norm = norm * inverse * inverse
    first_cross = total(moments[1:2, :]) / COUNT * inverse * inverse
    alpha = first_cross + SHIFT * first_norm
    rest = alpha - SHIFT
    beta = jnp.sqrt(
        total(moments[2:3, :]) / COUNT * inverse * inverse
        - 2.0 * rest * first_cross
        + rest * rest * first_norm
        + EPS
    )
    z = gap[...] * y[...] - jnp.sum(parts[...], axis=0)
    q_1 = x[...] * inverse
    scale = inverse / beta
    q_2 = (y[...] - rest * x[...]) * scale
    u = (z - rest * y[...]) * scale - beta * q_1
    u_out[...] = u
    q_out[...] = q_2
    lane = lax.broadcasted_iota(jnp.int32, (1, 128), 1)
    row = jnp.where(lane < 32, total(u * u), total(u * q_2))
    row = jnp.where(lane < 64, row, jnp.where(lane < 96, total(q_2 * q_2), total(q_1 * q_2)))
    message[...] = jnp.broadcast_to(row[None], message.shape)
    scalars[...] = jnp.where(lane < 64, alpha, beta)


def fold_body(parts, message):
    row = jnp.sum(parts[...], axis=0)
    message[...] = jnp.broadcast_to(row[None], message.shape)


def finish_body(parts, u, q_2, scalars, out, coefficients):
    row = jnp.sum(parts[...], axis=0) / COUNT
    uu, uq, qq, oq = row[:, 0:1], row[:, 32:33], row[:, 64:65], row[:, 96:97]
    beta_1 = scalars[:, 64:65]
    alpha = uq + beta_1 * oq + SHIFT * qq
    rest = alpha - SHIFT
    beta = jnp.sqrt(uu - 2.0 * rest * uq + rest * rest * qq + EPS)
    value = (u[...] - rest * q_2[...]) / beta
    out[0:16, :] = value[:, 0:64]
    out[16:32, :] = value[:, 64:128]
    coefficients[0] = scalars[0, 0]
    coefficients[1] = scalars[0, 64]
    coefficients[2] = alpha[0, 0]
    coefficients[3] = beta[0, 0]


def shards(excitons, valence_energy, conduction_energy, psi_valence, psi_conduction, screened):
    x, gap, first, pair = pl.pallas_call(
        start_body,
        out_shape=tuple(
            jax.ShapeDtypeStruct(shape, F32)
            for shape in [(16, 128), (16, 128), (32, 48, 128), (320, 128)]
        ),
        in_specs=[pl.BlockSpec(memory_space=pltpu.HBM)] * 5,
        out_specs=(pl.BlockSpec(memory_space=pltpu.VMEM),) * 4,
        scratch_shapes=[
            pltpu.VMEM((32, 64), F32),
            pltpu.VMEM((32, 256), F32),
            pltpu.VMEM((1, 64), F32),
            pltpu.VMEM((1, 32), F32),
            pltpu.SemaphoreType.DMA((5,)),
        ],
        name="start",
        compiler_params=pltpu.CompilerParams(vmem_limit_bytes=32 * 1024 * 1024),
    )(
        *(
            pltpu.with_memory_space_constraint(value, pltpu.HBM)
            for value in (
                excitons.T,
                psi_valence.T,
                valence_energy[None],
                conduction_energy[None],
                screened,
            )
        )
    )
    first = exchange(first, COL)
    panel_conduction = lax.all_gather(psi_conduction.T, ROW, axis=0, tiled=True)
    panel_conduction = panel_conduction.reshape(32, 2, 16, 128)

    pair = lax.all_gather(pair, "row_1", axis=0)
    (second,) = call(spread_body, [(32, 32, 128)], "spread")(pair)
    panel_conduction, second = lax.optimization_barrier((panel_conduction, second))

    def returned(partial):
        partials = lax.all_gather(partial, "row_1", axis=0)
        (back,) = call(weigh_body, [(16, 32, 128)], "weigh")(
            partials, pair, first, second
        )
        back = exchange(back, ROW).reshape(8, 2, 32, 128)
        (kernel,) = call(conduct_body, [(32, 16, 128)], "conduct")(back, panel_conduction)
        return exchange(kernel, COL)

    (image,) = call(first_points_body, [(64, 128)], "points_one")(first, panel_conduction)
    image, second = lax.optimization_barrier((image, second))
    second = exchange(second, COL)
    image = lax.all_gather(image, ROW, axis=0, tiled=True).reshape(32, 2, 16, 128)
    (partial,) = call(first_partial_body, [(2, 256, 128)], "partial_one")(image, first, second)
    y, spread = call(update_body, [(16, 128), (32, 16, 128)], "update")(returned(partial), gap, x)

    y_rows = exchange(spread, COL)
    (image,) = call(second_points_body, [(8, 2, 40, 128)], "points_two")(
        first, y_rows, panel_conduction
    )
    image = exchange(image.reshape(16, 40, 128), ROW)
    partial, moments = call(second_partial_body, [(2, 256, 128), (8, 128)], "partial_two")(
        image, first, second
    )
    u, q_2, message, scalars = call(
        last_body, [(16, 128), (16, 128), (64, 1, 128), (1, 128)], "last"
    )(returned(partial), gap, x, y, moments)
    (message,) = call(fold_body, [(8, 1, 128)], "fold")(exchange(message, (*ROW, "col_0")))
    out, coefficients = call(finish_body, [(32, 64), (4,)], "finish", smem=(1,))(
        exchange(message, "col_1"), u, q_2, scalars
    )
    return out.T, coefficients


def solution(mesh):
    finer = Mesh(mesh.devices.reshape(8, 2, 4, 8), ("row_0", "row_1", "col_0", "col_1"))
    placed = (P(ROW, COL), P(ROW), P(COL), P(ROW, COL), P(COL, ROW), P(ROW, COL))
    return jax.shard_map(
        shards, mesh=finer, in_specs=placed, out_specs=(P(ROW, COL), P()), check_vma=False
    )
```

```python
import jax
import jax.numpy as jnp
from jax import lax
from jax.experimental import pallas as pl
from jax.experimental.pallas import tpu as pltpu
from jax.sharding import Mesh
from jax.sharding import PartitionSpec as P

NV = 1024
NC = 1024
COUNT = NV * NC
COL = ("col_0", "col_1")
ROW = ("row_0", "row_1")
EPS = 1e-06
SHIFT = 4.0
F32 = jnp.float32


def exchange(value, axis):
    return lax.all_to_all(value, axis, 0, 0, tiled=True)


def halves(value):
    upper = value.astype(jnp.bfloat16)
    return upper, (value - upper.astype(F32)).astype(jnp.bfloat16)


def dot_halves(a, b):
    (a_hi, a_lo), (b_hi, b_lo) = a, b
    return (
        jnp.dot(a_lo, b_hi, preferred_element_type=F32)
        + jnp.dot(a_hi, b_lo, preferred_element_type=F32)
        + jnp.dot(a_hi, b_hi, preferred_element_type=F32)
    )


def call(body, outs, name, smem=()):
    shapes = tuple(jax.ShapeDtypeStruct(s, F32) for s in outs)
    specs = tuple(
        pl.BlockSpec(memory_space=pltpu.SMEM if i in smem else pltpu.VMEM)
        for i in range(len(outs))
    )
    return pl.pallas_call(
        body,
        out_shape=shapes,
        out_specs=specs,
        name=name,
        compiler_params=pltpu.CompilerParams(vmem_limit_bytes=32 * 1024 * 1024),
    )


def mine(zero, one):
    return jnp.where(lax.axis_index("row_1") == 0, zero, one)


def start_body(
    block_in, panel_in, valence_in, conduction_in, screened_in, packed, gap, first, pair,
    block, panel, valence, conduction, tile, arrived, sent,
):
    moves = [
        pltpu.make_async_copy(source, target, arrived.at[i])
        for i, (source, target) in enumerate(
            [
                (block_in, block),
                (panel_in, panel),
                (valence_in, valence),
                (conduction_in, conduction),
                (screened_in, pair.at[64:320]),
            ]
        )
    ]
    for move in moves:
        move.start()
    for move in moves[:4]:
        move.wait()
    value = jnp.concatenate([block[0:16, :], block[16:32, :]], axis=1)
    packed[...] = value
    half = mine(panel[0:16, :], panel[16:32, :])
    tile[0:16, :] = value
    tile[16:32, :] = half[:, 0:128]
    tile[32:48, :] = half[:, 128:256]
    spreads = [pltpu.make_async_copy(tile, first.at[i], sent.at[i]) for i in range(32)]
    for spread in spreads:
        spread.start()
    rows = lax.broadcasted_iota(jnp.int32, (32, 32), 0)
    lanes = lax.broadcasted_iota(jnp.int32, (32, 32), 1)
    column = jnp.sum(jnp.where(rows == lanes, conduction[...], 0.0), axis=1, keepdims=True)
    half = lax.broadcasted_iota(jnp.int32, (16, 128), 1) < 64
    upper = jnp.where(half, column[0:16], column[16:32])
    gap[...] = upper - jnp.concatenate([valence[...], valence[...]], axis=1) - SHIFT
    pair[0:32, :] = panel[:, 0:128]
    pair[32:64, :] = panel[:, 128:256]
    moves[4].wait()
    for spread in spreads:
        spread.wait()


def points_of(rows, panel):
    rows = halves(rows.T)
    lo = dot_halves(rows, halves(panel[:, 0].reshape(512, 128)))
    hi = dot_halves(rows, halves(panel[:, 1].reshape(512, 128)))
    return lo[0:64] + hi[64:128]


def spread_body(pair, second):
    low = mine(pair[1, 0:16, :], pair[0, 16:32, :])
    high = mine(pair[1, 32:48, :], pair[0, 48:64, :])
    second[:, 0:16, :] = jnp.broadcast_to(low[None], (32, 16, 128))
    second[:, 16:32, :] = jnp.broadcast_to(high[None], (32, 16, 128))


def first_points_body(first, panel, out):
    out[...] = points_of(first[:, 0:16, :].reshape(512, 128), panel)


def second_points_body(first, y_rows, panel, out):
    x = first[:, 0:16, :].reshape(512, 128)
    y = y_rows[...].reshape(512, 128)
    sums = [jnp.sum(a * b, axis=0, keepdims=True) for a, b in ((x, x), (x, y), (y, y))]
    sums.append(jnp.zeros((5, 128), F32))
    image = points_of(y, panel)
    for core in range(2):
        at = 16 * core
        message = [image[at : at + 16], image[at + 32 : at + 48], *sums]
        message = jnp.concatenate(message, axis=0)
        out[:, core] = jnp.broadcast_to(message[None], (8, 40, 128))


def shared_panel(first, second):
    parts = [first[:, 16:32, :], first[:, 32:48, :], second[:, 0:16, :], second[:, 16:32, :]]
    return halves(jnp.concatenate([part.reshape(512, 128) for part in parts], axis=1))


def partial_points(image, first, second, out):
    points = dot_halves(halves(image.T), shared_panel(first, second)).T
    out[0] = mine(points[0:256], points[256:512])
    out[1] = mine(points[256:512], points[0:256])


def first_partial_body(image, first, second, out):
    image = mine(image[:, 0], image[:, 1]).reshape(512, 128)
    partial_points(image, first, second, out)


def second_partial_body(arrived, first, second, out, moments):
    partial_points(arrived[:, 0:32, :].reshape(512, 128), first, second, out)
    moments[...] = jnp.sum(arrived[:, 32:40, :], axis=0)


def weigh_body(partials, pair, first, second, out):
    zero = (partials[0, 0] + partials[1, 0]) * pair[0, 64:320, :]
    one = (partials[0, 1] + partials[1, 1]) * pair[1, 64:320, :]
    weighted = jnp.concatenate([mine(zero, one), mine(one, zero)], axis=0)
    back = dot_halves(shared_panel(first, second), halves(weighted))
    out[...] = back.reshape(16, 32, 128)


def conduct_body(parts, panel, out):
    sums = jnp.sum(parts[...], axis=0)
    back = jnp.stack([sums[0].reshape(2, 16, 128), sums[1].reshape(2, 16, 128)], axis=1)
    back = back.reshape(64, 128).T
    zero = jnp.zeros_like(back)
    lo = dot_halves(
        halves(panel[:, 0].reshape(512, 128)), halves(jnp.concatenate([back, zero], axis=1))
    )
    hi = dot_halves(
        halves(panel[:, 1].reshape(512, 128)), halves(jnp.concatenate([zero, back], axis=1))
    )
    out[...] = (lo + hi).reshape(32, 16, 128)


def update_body(parts, gap, x, packed, spread):
    value = gap[...] * x[...] - jnp.sum(parts[...], axis=0)
    packed[...] = value
    spread[...] = jnp.broadcast_to(value[None], spread.shape)


def total(value):
    return jnp.sum(jnp.sum(value, axis=0, keepdims=True), axis=1, keepdims=True)


def last_body(parts, gap, x, y, moments, u_out, q_out, message, scalars):
    norm = total(moments[0:1, :]) / COUNT
    inverse = 1.0 / jnp.sqrt(norm + EPS)
    first_norm = norm * inverse * inverse
    first_cross = total(moments[1:2, :]) / COUNT * inverse * inverse
    alpha = first_cross + SHIFT * first_norm
    rest = alpha - SHIFT
    beta = jnp.sqrt(
        total(moments[2:3, :]) / COUNT * inverse * inverse
        - 2.0 * rest * first_cross
        + rest * rest * first_norm
        + EPS
    )
    z = gap[...] * y[...] - jnp.sum(parts[...], axis=0)
    q_1 = x[...] * inverse
    scale = inverse / beta
    q_2 = (y[...] - rest * x[...]) * scale
    u = (z - rest * y[...]) * scale - beta * q_1
    u_out[...] = u
    q_out[...] = q_2
    lane = lax.broadcasted_iota(jnp.int32, (1, 128), 1)
    row = jnp.where(lane < 32, total(u * u), total(u * q_2))
    row = jnp.where(lane < 64, row, jnp.where(lane < 96, total(q_2 * q_2), total(q_1 * q_2)))
    message[...] = jnp.broadcast_to(row[None], message.shape)
    scalars[...] = jnp.where(lane < 64, alpha, beta)


def fold_body(parts, message):
    row = jnp.sum(parts[...], axis=0)
    message[...] = jnp.broadcast_to(row[None], message.shape)


def finish_body(parts, u, q_2, scalars, out, coefficients):
    row = jnp.sum(parts[...], axis=0) / COUNT
    uu, uq, qq, oq = row[:, 0:1], row[:, 32:33], row[:, 64:65], row[:, 96:97]
    beta_1 = scalars[:, 64:65]
    alpha = uq + beta_1 * oq + SHIFT * qq
    rest = alpha - SHIFT
    beta = jnp.sqrt(uu - 2.0 * rest * uq + rest * rest * qq + EPS)
    value = (u[...] - rest * q_2[...]) / beta
    out[0:16, :] = value[:, 0:64]
    out[16:32, :] = value[:, 64:128]
    coefficients[0] = scalars[0, 0]
    coefficients[1] = scalars[0, 64]
    coefficients[2] = alpha[0, 0]
    coefficients[3] = beta[0, 0]


def shards(excitons, valence_energy, conduction_energy, psi_valence, psi_conduction, screened):
    x, gap, first, pair = pl.pallas_call(
        start_body,
        out_shape=tuple(
            jax.ShapeDtypeStruct(shape, F32)
            for shape in [(16, 128), (16, 128), (32, 48, 128), (320, 128)]
        ),
        in_specs=[pl.BlockSpec(memory_space=pltpu.HBM)] * 5,
        out_specs=tuple(
            pl.BlockSpec(memory_space=pltpu.HBM if i == 2 else pltpu.VMEM) for i in range(4)
        ),
        scratch_shapes=[
            pltpu.VMEM((32, 64), F32),
            pltpu.VMEM((32, 256), F32),
            pltpu.VMEM((1, 64), F32),
            pltpu.VMEM((1, 32), F32),
            pltpu.VMEM((48, 128), F32),
            pltpu.SemaphoreType.DMA((5,)),
            pltpu.SemaphoreType.DMA((32,)),
        ],
        name="start",
        compiler_params=pltpu.CompilerParams(vmem_limit_bytes=32 * 1024 * 1024),
    )(
        *(
            pltpu.with_memory_space_constraint(value, pltpu.HBM)
            for value in (
                excitons.T,
                psi_valence.T,
                valence_energy[None],
                conduction_energy[None],
                screened,
            )
        )
    )
    first = exchange(first, COL)
    panel_conduction = lax.all_gather(psi_conduction.T, ROW, axis=0, tiled=True)
    panel_conduction = panel_conduction.reshape(32, 2, 16, 128)

    pair = lax.all_gather(pair, "row_1", axis=0)
    (second,) = call(spread_body, [(32, 32, 128)], "spread")(pair)
    panel_conduction, second = lax.optimization_barrier((panel_conduction, second))

    def returned(partial):
        partials = lax.all_gather(partial, "row_1", axis=0)
        (back,) = call(weigh_body, [(16, 32, 128)], "weigh")(
            partials, pair, first, second
        )
        back = exchange(back, ROW).reshape(8, 2, 32, 128)
        (kernel,) = call(conduct_body, [(32, 16, 128)], "conduct")(back, panel_conduction)
        return exchange(kernel, COL)

    (image,) = call(first_points_body, [(64, 128)], "points_one")(first, panel_conduction)
    image, second = lax.optimization_barrier((image, second))
    second = exchange(second, COL)
    image = lax.all_gather(image, ROW, axis=0, tiled=True).reshape(32, 2, 16, 128)
    (partial,) = call(first_partial_body, [(2, 256, 128)], "partial_one")(image, first, second)
    y, spread = call(update_body, [(16, 128), (32, 16, 128)], "update")(returned(partial), gap, x)

    y_rows = exchange(spread, COL)
    (image,) = call(second_points_body, [(8, 2, 40, 128)], "points_two")(
        first, y_rows, panel_conduction
    )
    image = exchange(image.reshape(16, 40, 128), ROW)
    partial, moments = call(second_partial_body, [(2, 256, 128), (8, 128)], "partial_two")(
        image, first, second
    )
    u, q_2, message, scalars = call(
        last_body, [(16, 128), (16, 128), (8, 1, 128), (1, 128)], "last"
    )(returned(partial), gap, x, y, moments)
    (message,) = call(fold_body, [(64, 1, 128)], "fold")(exchange(message, ("row_1", "col_0")))
    out, coefficients = call(finish_body, [(32, 64), (4,)], "finish", smem=(1,))(
        exchange(message, ("row_0", "col_1")), u, q_2, scalars
    )
    return out.T, coefficients


def solution(mesh):
    finer = Mesh(mesh.devices.reshape(8, 2, 4, 8), ("row_0", "row_1", "col_0", "col_1"))
    placed = (P(ROW, COL), P(ROW), P(COL), P(ROW, COL), P(COL, ROW), P(ROW, COL))
    return jax.shard_map(
        shards, mesh=finer, in_specs=placed, out_specs=(P(ROW, COL), P()), check_vma=False
    )
```

```python
import jax
import jax.numpy as jnp
from jax import lax
from jax.experimental import pallas as pl
from jax.experimental.pallas import tpu as pltpu
from jax.sharding import Mesh
from jax.sharding import PartitionSpec as P

NV = 1024
NC = 1024
COUNT = NV * NC
COL = ("col_0", "col_1")
ROW = ("row_0", "row_1")
CORE_MAJOR = ("row_1", "row_0")
EPS = 1e-06
SHIFT = 4.0
F32 = jnp.float32


def exchange(value, axis):
    return lax.all_to_all(value, axis, 0, 0, tiled=True)


def halves(value):
    upper = value.astype(jnp.bfloat16)
    return upper, (value - upper.astype(F32)).astype(jnp.bfloat16)


def dot_halves(a, b):
    (a_hi, a_lo), (b_hi, b_lo) = a, b
    return (
        jnp.dot(a_lo, b_hi, preferred_element_type=F32)
        + jnp.dot(a_hi, b_lo, preferred_element_type=F32)
        + jnp.dot(a_hi, b_hi, preferred_element_type=F32)
    )


def call(body, outs, name, smem=()):
    shapes = tuple(jax.ShapeDtypeStruct(s, F32) for s in outs)
    specs = tuple(
        pl.BlockSpec(memory_space=pltpu.SMEM if i in smem else pltpu.VMEM)
        for i in range(len(outs))
    )
    return pl.pallas_call(
        body,
        out_shape=shapes,
        out_specs=specs,
        name=name,
        compiler_params=pltpu.CompilerParams(vmem_limit_bytes=32 * 1024 * 1024),
    )


def mine(zero, one):
    return jnp.where(lax.axis_index("row_1") == 0, zero, one)


def spread_half(out, at, low, high):
    out[:, at : at + 16, :] = jnp.broadcast_to(low[None], (32, 16, 128))
    out[:, at + 16 : at + 32, :] = jnp.broadcast_to(high[None], (32, 16, 128))


def start_body(
    block_in, panel_in, valence_in, conduction_in, screened_in, packed, gap, first, pair,
    block, panel, valence, conduction, arrived,
):
    moves = [
        pltpu.make_async_copy(source, target, arrived.at[i])
        for i, (source, target) in enumerate(
            [
                (block_in, block),
                (panel_in, panel),
                (valence_in, valence),
                (conduction_in, conduction),
                (screened_in, pair.at[64:320]),
            ]
        )
    ]
    for move in moves:
        move.start()
    for move in moves[:4]:
        move.wait()
    value = jnp.concatenate([block[0:16, :], block[16:32, :]], axis=1)
    packed[...] = value
    first[:, 0:16, :] = jnp.broadcast_to(value[None], (32, 16, 128))
    half = mine(panel[0:16, :], panel[16:32, :])
    spread_half(first, 16, half[:, 0:128], half[:, 128:256])
    rows = lax.broadcasted_iota(jnp.int32, (32, 32), 0)
    lanes = lax.broadcasted_iota(jnp.int32, (32, 32), 1)
    column = jnp.sum(jnp.where(rows == lanes, conduction[...], 0.0), axis=1, keepdims=True)
    half = lax.broadcasted_iota(jnp.int32, (16, 128), 1) < 64
    upper = jnp.where(half, column[0:16], column[16:32])
    gap[...] = upper - jnp.concatenate([valence[...], valence[...]], axis=1) - SHIFT
    pair[0:32, :] = panel[:, 0:128]
    pair[32:64, :] = panel[:, 128:256]
    moves[4].wait()


def points_of(rows, panel):
    rows = halves(rows.T)
    lo = dot_halves(rows, halves(panel[:, 0].reshape(512, 128)))
    hi = dot_halves(rows, halves(panel[:, 1].reshape(512, 128)))
    return lo[0:64] + hi[64:128]


def spread_body(pair, second):
    low = mine(pair[1, 0:16, :], pair[0, 16:32, :])
    spread_half(second, 0, low, mine(pair[1, 32:48, :], pair[0, 48:64, :]))


def first_points_body(first, panel, out):
    out[...] = points_of(first[:, 0:16, :].reshape(512, 128), panel)


def second_points_body(first, y_rows, panel, out):
    x = first[:, 0:16, :].reshape(512, 128)
    y = y_rows[...].reshape(512, 128)
    sums = [jnp.sum(a * b, axis=0, keepdims=True) for a, b in ((x, x), (x, y), (y, y))]
    sums.append(jnp.zeros((5, 128), F32))
    image = points_of(y, panel)
    for core in range(2):
        at = 16 * core
        message = [image[at : at + 16], image[at + 32 : at + 48], *sums]
        message = jnp.concatenate(message, axis=0)
        out[core] = jnp.broadcast_to(message[None], (8, 40, 128))


def shared_panel(first, second):
    parts = [first[:, 16:32, :], first[:, 32:48, :], second[:, 0:16, :], second[:, 16:32, :]]
    return halves(jnp.concatenate([part.reshape(512, 128) for part in parts], axis=1))


def partial_points(image, first, second, out):
    points = dot_halves(halves(image.T), shared_panel(first, second)).T
    out[0] = mine(points[0:256], points[256:512])
    out[1] = mine(points[256:512], points[0:256])


def first_partial_body(image, first, second, out):
    image = mine(image[:, 0], image[:, 1]).reshape(512, 128)
    partial_points(image, first, second, out)


def second_partial_body(arrived, first, second, out, moments):
    image = jnp.stack([arrived[0, :, 0:32, :], arrived[1, :, 0:32, :]], axis=1)
    partial_points(image.reshape(512, 128), first, second, out)
    moments[...] = jnp.sum(arrived[0, :, 32:40, :] + arrived[1, :, 32:40, :], axis=0)


def weigh_body(partials, pair, first, second, out):
    zero = (partials[0, 0] + partials[1, 0]) * pair[0, 64:320, :]
    one = (partials[0, 1] + partials[1, 1]) * pair[1, 64:320, :]
    weighted = jnp.concatenate([mine(zero, one), mine(one, zero)], axis=0)
    back = dot_halves(shared_panel(first, second), halves(weighted))
    back = back.reshape(8, 2, 32, 128)
    out[0] = back[:, 0]
    out[1] = back[:, 1]


def conduct_body(parts, panel, out):
    sums = jnp.sum(parts[...], axis=1)
    back = jnp.stack([sums[0].reshape(2, 16, 128), sums[1].reshape(2, 16, 128)], axis=1)
    back = back.reshape(64, 128).T
    zero = jnp.zeros_like(back)
    lo = dot_halves(
        halves(panel[:, 0].reshape(512, 128)), halves(jnp.concatenate([back, zero], axis=1))
    )
    hi = dot_halves(
        halves(panel[:, 1].reshape(512, 128)), halves(jnp.concatenate([zero, back], axis=1))
    )
    out[...] = (lo + hi).reshape(32, 16, 128)


def update_body(parts, gap, x, packed, spread):
    value = gap[...] * x[...] - jnp.sum(parts[...], axis=0)
    packed[...] = value
    spread[...] = jnp.broadcast_to(value[None], spread.shape)


def total(value):
    return jnp.sum(jnp.sum(value, axis=0, keepdims=True), axis=1, keepdims=True)


def last_body(parts, gap, x, y, moments, u_out, q_out, message, scalars):
    norm = total(moments[0:1, :]) / COUNT
    inverse = 1.0 / jnp.sqrt(norm + EPS)
    first_norm = norm * inverse * inverse
    first_cross = total(moments[1:2, :]) / COUNT * inverse * inverse
    alpha = first_cross + SHIFT * first_norm
    rest = alpha - SHIFT
    beta = jnp.sqrt(
        total(moments[2:3, :]) / COUNT * inverse * inverse
        - 2.0 * rest * first_cross
        + rest * rest * first_norm
        + EPS
    )
    z = gap[...] * y[...] - jnp.sum(parts[...], axis=0)
    q_1 = x[...] * inverse
    scale = inverse / beta
    q_2 = (y[...] - rest * x[...]) * scale
    u = (z - rest * y[...]) * scale - beta * q_1
    u_out[...] = u
    q_out[...] = q_2
    lane = lax.broadcasted_iota(jnp.int32, (1, 128), 1)
    row = jnp.where(lane < 32, total(u * u), total(u * q_2))
    row = jnp.where(lane < 64, row, jnp.where(lane < 96, total(q_2 * q_2), total(q_1 * q_2)))
    message[...] = jnp.broadcast_to(row[None], message.shape)
    scalars[...] = jnp.where(lane < 64, alpha, beta)


def fold_body(parts, message):
    row = jnp.sum(parts[...], axis=0)
    message[...] = jnp.broadcast_to(row[None], message.shape)


def finish_body(parts, u, q_2, scalars, out, coefficients):
    row = jnp.sum(parts[...], axis=0) / COUNT
    uu, uq, qq, oq = row[:, 0:1], row[:, 32:33], row[:, 64:65], row[:, 96:97]
    beta_1 = scalars[:, 64:65]
    alpha = uq + beta_1 * oq + SHIFT * qq
    rest = alpha - SHIFT
    beta = jnp.sqrt(uu - 2.0 * rest * uq + rest * rest * qq + EPS)
    value = (u[...] - rest * q_2[...]) / beta
    out[0:16, :] = value[:, 0:64]
    out[16:32, :] = value[:, 64:128]
    coefficients[0] = scalars[0, 0]
    coefficients[1] = scalars[0, 64]
    coefficients[2] = alpha[0, 0]
    coefficients[3] = beta[0, 0]


def shards(excitons, valence_energy, conduction_energy, psi_valence, psi_conduction, screened):
    x, gap, first, pair = pl.pallas_call(
        start_body,
        out_shape=tuple(
            jax.ShapeDtypeStruct(shape, F32)
            for shape in [(16, 128), (16, 128), (32, 48, 128), (320, 128)]
        ),
        in_specs=[pl.BlockSpec(memory_space=pltpu.HBM)] * 5,
        out_specs=(pl.BlockSpec(memory_space=pltpu.VMEM),) * 4,
        scratch_shapes=[
            pltpu.VMEM((32, 64), F32),
            pltpu.VMEM((32, 256), F32),
            pltpu.VMEM((1, 64), F32),
            pltpu.VMEM((1, 32), F32),
            pltpu.SemaphoreType.DMA((5,)),
        ],
        name="start",
        compiler_params=pltpu.CompilerParams(vmem_limit_bytes=32 * 1024 * 1024),
    )(
        *(
            pltpu.with_memory_space_constraint(value, pltpu.HBM)
            for value in (
                excitons.T,
                psi_valence.T,
                valence_energy[None],
                conduction_energy[None],
                screened,
            )
        )
    )
    first = exchange(first, COL)
    panel_conduction = lax.all_gather(psi_conduction.T, ROW, axis=0, tiled=True)
    panel_conduction = panel_conduction.reshape(32, 2, 16, 128)

    pair = lax.all_gather(pair, "row_1", axis=0)
    (second,) = call(spread_body, [(32, 32, 128)], "spread")(pair)
    panel_conduction, second = lax.optimization_barrier((panel_conduction, second))

    def returned(partial):
        partials = lax.all_gather(partial, "row_1", axis=0)
        (back,) = call(weigh_body, [(2, 8, 32, 128)], "weigh")(
            partials, pair, first, second
        )
        back = exchange(back.reshape(16, 32, 128), CORE_MAJOR).reshape(2, 8, 32, 128)
        (kernel,) = call(conduct_body, [(32, 16, 128)], "conduct")(back, panel_conduction)
        return exchange(kernel, COL)

    (image,) = call(first_points_body, [(64, 128)], "points_one")(first, panel_conduction)
    image, second = lax.optimization_barrier((image, second))
    second = exchange(second, COL)
    image = lax.all_gather(image, ROW, axis=0, tiled=True).reshape(32, 2, 16, 128)
    (partial,) = call(first_partial_body, [(2, 256, 128)], "partial_one")(image, first, second)
    y, spread = call(update_body, [(16, 128), (32, 16, 128)], "update")(returned(partial), gap, x)

    y_rows = exchange(spread, COL)
    (image,) = call(second_points_body, [(2, 8, 40, 128)], "points_two")(
        first, y_rows, panel_conduction
    )
    image = exchange(image.reshape(16, 40, 128), CORE_MAJOR).reshape(2, 8, 40, 128)
    partial, moments = call(second_partial_body, [(2, 256, 128), (8, 128)], "partial_two")(
        image, first, second
    )
    u, q_2, message, scalars = call(
        last_body, [(16, 128), (16, 128), (64, 1, 128), (1, 128)], "last"
    )(returned(partial), gap, x, y, moments)
    (message,) = call(fold_body, [(8, 1, 128)], "fold")(exchange(message, (*CORE_MAJOR, "col_0")))
    out, coefficients = call(finish_body, [(32, 64), (4,)], "finish", smem=(1,))(
        exchange(message, "col_1"), u, q_2, scalars
    )
    return out.T, coefficients


def solution(mesh):
    finer = Mesh(mesh.devices.reshape(8, 2, 4, 8), ("row_0", "row_1", "col_0", "col_1"))
    placed = (P(ROW, COL), P(ROW), P(COL), P(ROW, COL), P(COL, ROW), P(ROW, COL))
    return jax.shard_map(
        shards, mesh=finer, in_specs=placed, out_specs=(P(ROW, COL), P()), check_vma=False
    )
```

```python
import jax
import jax.numpy as jnp
from jax import lax
from jax.experimental import pallas as pl
from jax.experimental.pallas import tpu as pltpu
from jax.sharding import Mesh
from jax.sharding import PartitionSpec as P

NV = 1024
NC = 1024
COUNT = NV * NC
COL = ("col_0", "col_1")
ROW = ("row_0", "row_1")
CORE_MAJOR = ("row_1", "row_0")
Z_MAJOR = ("col_1", "col_0")
EPS = 1e-06
SHIFT = 4.0
F32 = jnp.float32


def exchange(value, axis):
    return lax.all_to_all(value, axis, 0, 0, tiled=True)


def halves(value):
    upper = value.astype(jnp.bfloat16)
    return upper, (value - upper.astype(F32)).astype(jnp.bfloat16)


def dot_halves(a, b):
    (a_hi, a_lo), (b_hi, b_lo) = a, b
    return (
        jnp.dot(a_lo, b_hi, preferred_element_type=F32)
        + jnp.dot(a_hi, b_lo, preferred_element_type=F32)
        + jnp.dot(a_hi, b_hi, preferred_element_type=F32)
    )


def call(body, outs, name, smem=()):
    shapes = tuple(jax.ShapeDtypeStruct(s, F32) for s in outs)
    specs = tuple(
        pl.BlockSpec(memory_space=pltpu.SMEM if i in smem else pltpu.VMEM)
        for i in range(len(outs))
    )
    return pl.pallas_call(
        body,
        out_shape=shapes,
        out_specs=specs,
        name=name,
        compiler_params=pltpu.CompilerParams(vmem_limit_bytes=32 * 1024 * 1024),
    )


def mine(zero, one):
    return jnp.where(lax.axis_index("row_1") == 0, zero, one)


def spread_half(out, at, low, high):
    out[:, at : at + 16, :] = jnp.broadcast_to(low[None], (32, 16, 128))
    out[:, at + 16 : at + 32, :] = jnp.broadcast_to(high[None], (32, 16, 128))


def start_body(
    block_in, panel_in, valence_in, conduction_in, screened_in, packed, gap, first, pair,
    block, panel, valence, conduction, arrived,
):
    moves = [
        pltpu.make_async_copy(source, target, arrived.at[i])
        for i, (source, target) in enumerate(
            [
                (block_in, block),
                (panel_in, panel),
                (valence_in, valence),
                (conduction_in, conduction),
                (screened_in, pair.at[64:320]),
            ]
        )
    ]
    for move in moves:
        move.start()
    for move in moves[:4]:
        move.wait()
    value = jnp.concatenate([block[0:16, :], block[16:32, :]], axis=1)
    packed[...] = value
    first[:, 0:16, :] = jnp.broadcast_to(value[None], (32, 16, 128))
    half = mine(panel[0:16, :], panel[16:32, :])
    spread_half(first, 16, half[:, 0:128], half[:, 128:256])
    rows = lax.broadcasted_iota(jnp.int32, (32, 32), 0)
    lanes = lax.broadcasted_iota(jnp.int32, (32, 32), 1)
    column = jnp.sum(jnp.where(rows == lanes, conduction[...], 0.0), axis=1, keepdims=True)
    half = lax.broadcasted_iota(jnp.int32, (16, 128), 1) < 64
    upper = jnp.where(half, column[0:16], column[16:32])
    gap[...] = upper - jnp.concatenate([valence[...], valence[...]], axis=1) - SHIFT
    pair[0:32, :] = panel[:, 0:128]
    pair[32:64, :] = panel[:, 128:256]
    moves[4].wait()


def points_of(rows, panel):
    rows = halves(rows.T)
    lo = dot_halves(rows, halves(panel[:, 0].reshape(512, 128)))
    hi = dot_halves(rows, halves(panel[:, 1].reshape(512, 128)))
    return lo[0:64] + hi[64:128]


def spread_body(pair, second):
    low = mine(pair[1, 0:16, :], pair[0, 16:32, :])
    spread_half(second, 0, low, mine(pair[1, 32:48, :], pair[0, 48:64, :]))


def first_points_body(first, panel, out):
    out[...] = points_of(first[:, 0:16, :].reshape(512, 128), panel)


def second_points_body(first, y_rows, panel, out):
    x = first[:, 0:16, :].reshape(512, 128)
    y = jnp.stack([y_rows[:, at] for at in range(4)], axis=0).reshape(512, 128)
    sums = [jnp.sum(a * b, axis=0, keepdims=True) for a, b in ((x, x), (x, y), (y, y))]
    sums.append(jnp.zeros((5, 128), F32))
    image = points_of(y, panel)
    for core in range(2):
        at = 16 * core
        message = [image[at : at + 16], image[at + 32 : at + 48], *sums]
        message = jnp.concatenate(message, axis=0)
        out[core] = jnp.broadcast_to(message[None], (8, 40, 128))


def shared_panel(first, second):
    parts = [first[:, 16:32, :], first[:, 32:48, :], second[:, 0:16, :], second[:, 16:32, :]]
    return halves(jnp.concatenate([part.reshape(512, 128) for part in parts], axis=1))


def partial_points(image, first, second, out):
    points = dot_halves(halves(image.T), shared_panel(first, second)).T
    out[0] = mine(points[0:256], points[256:512])
    out[1] = mine(points[256:512], points[0:256])


def first_partial_body(image, first, second, out):
    image = mine(image[:, 0], image[:, 1]).reshape(512, 128)
    partial_points(image, first, second, out)


def second_partial_body(arrived, first, second, out, moments):
    image = jnp.stack([arrived[0, :, 0:32, :], arrived[1, :, 0:32, :]], axis=1)
    partial_points(image.reshape(512, 128), first, second, out)
    moments[...] = jnp.sum(arrived[0, :, 32:40, :] + arrived[1, :, 32:40, :], axis=0)


def weigh_body(partials, pair, first, second, out):
    zero = (partials[0, 0] + partials[1, 0]) * pair[0, 64:320, :]
    one = (partials[0, 1] + partials[1, 1]) * pair[1, 64:320, :]
    weighted = jnp.concatenate([mine(zero, one), mine(one, zero)], axis=0)
    back = dot_halves(shared_panel(first, second), halves(weighted))
    back = back.reshape(8, 2, 32, 128)
    out[0] = back[:, 0]
    out[1] = back[:, 1]


def conduct_body(parts, panel, out):
    sums = jnp.sum(parts[...], axis=1)
    back = jnp.stack([sums[0].reshape(2, 16, 128), sums[1].reshape(2, 16, 128)], axis=1)
    back = back.reshape(64, 128).T
    zero = jnp.zeros_like(back)
    lo = dot_halves(
        halves(panel[:, 0].reshape(512, 128)), halves(jnp.concatenate([back, zero], axis=1))
    )
    hi = dot_halves(
        halves(panel[:, 1].reshape(512, 128)), halves(jnp.concatenate([zero, back], axis=1))
    )
    value = (lo + hi).reshape(4, 8, 16, 128)
    for at in range(4):
        out[:, at] = value[at]


def update_body(parts, gap, x, packed, spread):
    value = gap[...] * x[...] - jnp.sum(parts[...], axis=0)
    packed[...] = value
    spread[...] = jnp.broadcast_to(value[None], spread.shape)


def total(value):
    return jnp.sum(jnp.sum(value, axis=0, keepdims=True), axis=1, keepdims=True)


def last_body(parts, gap, x, y, moments, u_out, q_out, message, scalars):
    norm = total(moments[0:1, :]) / COUNT
    inverse = 1.0 / jnp.sqrt(norm + EPS)
    first_norm = norm * inverse * inverse
    first_cross = total(moments[1:2, :]) / COUNT * inverse * inverse
    alpha = first_cross + SHIFT * first_norm
    rest = alpha - SHIFT
    beta = jnp.sqrt(
        total(moments[2:3, :]) / COUNT * inverse * inverse
        - 2.0 * rest * first_cross
        + rest * rest * first_norm
        + EPS
    )
    z = gap[...] * y[...] - jnp.sum(parts[...], axis=0)
    q_1 = x[...] * inverse
    scale = inverse / beta
    q_2 = (y[...] - rest * x[...]) * scale
    u = (z - rest * y[...]) * scale - beta * q_1
    u_out[...] = u
    q_out[...] = q_2
    lane = lax.broadcasted_iota(jnp.int32, (1, 128), 1)
    row = jnp.where(lane < 32, total(u * u), total(u * q_2))
    row = jnp.where(lane < 64, row, jnp.where(lane < 96, total(q_2 * q_2), total(q_1 * q_2)))
    message[...] = jnp.broadcast_to(row[None], message.shape)
    scalars[...] = jnp.where(lane < 64, alpha, beta)


def fold_body(parts, message):
    row = jnp.sum(parts[...], axis=0)
    message[...] = jnp.broadcast_to(row[None], message.shape)


def finish_body(parts, u, q_2, scalars, out, coefficients):
    row = jnp.sum(parts[...], axis=0) / COUNT
    uu, uq, qq, oq = row[:, 0:1], row[:, 32:33], row[:, 64:65], row[:, 96:97]
    beta_1 = scalars[:, 64:65]
    alpha = uq + beta_1 * oq + SHIFT * qq
    rest = alpha - SHIFT
    beta = jnp.sqrt(uu - 2.0 * rest * uq + rest * rest * qq + EPS)
    value = (u[...] - rest * q_2[...]) / beta
    out[0:16, :] = value[:, 0:64]
    out[16:32, :] = value[:, 64:128]
    coefficients[0] = scalars[0, 0]
    coefficients[1] = scalars[0, 64]
    coefficients[2] = alpha[0, 0]
    coefficients[3] = beta[0, 0]


def shards(excitons, valence_energy, conduction_energy, psi_valence, psi_conduction, screened):
    x, gap, first, pair = pl.pallas_call(
        start_body,
        out_shape=tuple(
            jax.ShapeDtypeStruct(shape, F32)
            for shape in [(16, 128), (16, 128), (32, 48, 128), (320, 128)]
        ),
        in_specs=[pl.BlockSpec(memory_space=pltpu.HBM)] * 5,
        out_specs=(pl.BlockSpec(memory_space=pltpu.VMEM),) * 4,
        scratch_shapes=[
            pltpu.VMEM((32, 64), F32),
            pltpu.VMEM((32, 256), F32),
            pltpu.VMEM((1, 64), F32),
            pltpu.VMEM((1, 32), F32),
            pltpu.SemaphoreType.DMA((5,)),
        ],
        name="start",
        compiler_params=pltpu.CompilerParams(vmem_limit_bytes=32 * 1024 * 1024),
    )(
        *(
            pltpu.with_memory_space_constraint(value, pltpu.HBM)
            for value in (
                excitons.T,
                psi_valence.T,
                valence_energy[None],
                conduction_energy[None],
                screened,
            )
        )
    )
    first = exchange(first, COL)
    panel_conduction = lax.all_gather(psi_conduction.T, ROW, axis=0, tiled=True)
    panel_conduction = panel_conduction.reshape(32, 2, 16, 128)

    pair = lax.all_gather(pair, "row_1", axis=0)
    (second,) = call(spread_body, [(32, 32, 128)], "spread")(pair)
    panel_conduction, second = lax.optimization_barrier((panel_conduction, second))

    def returned(partial):
        partials = lax.all_gather(partial, "row_1", axis=0)
        (back,) = call(weigh_body, [(2, 8, 32, 128)], "weigh")(
            partials, pair, first, second
        )
        back = exchange(back.reshape(16, 32, 128), CORE_MAJOR).reshape(2, 8, 32, 128)
        (kernel,) = call(conduct_body, [(8, 4, 16, 128)], "conduct")(back, panel_conduction)
        return exchange(kernel.reshape(32, 16, 128), Z_MAJOR)

    (image,) = call(first_points_body, [(64, 128)], "points_one")(first, panel_conduction)
    image, second = lax.optimization_barrier((image, second))
    second = exchange(second, COL)
    image = lax.all_gather(image, ROW, axis=0, tiled=True).reshape(32, 2, 16, 128)
    (partial,) = call(first_partial_body, [(2, 256, 128)], "partial_one")(image, first, second)
    y, spread = call(update_body, [(16, 128), (32, 16, 128)], "update")(returned(partial), gap, x)

    y_rows = exchange(spread, Z_MAJOR).reshape(8, 4, 16, 128)
    (image,) = call(second_points_body, [(2, 8, 40, 128)], "points_two")(
        first, y_rows, panel_conduction
    )
    image = exchange(image.reshape(16, 40, 128), CORE_MAJOR).reshape(2, 8, 40, 128)
    partial, moments = call(second_partial_body, [(2, 256, 128), (8, 128)], "partial_two")(
        image, first, second
    )
    u, q_2, message, scalars = call(
        last_body, [(16, 128), (16, 128), (64, 1, 128), (1, 128)], "last"
    )(returned(partial), gap, x, y, moments)
    (message,) = call(fold_body, [(8, 1, 128)], "fold")(exchange(message, (*CORE_MAJOR, "col_0")))
    out, coefficients = call(finish_body, [(32, 64), (4,)], "finish", smem=(1,))(
        exchange(message, "col_1"), u, q_2, scalars
    )
    return out.T, coefficients


def solution(mesh):
    finer = Mesh(mesh.devices.reshape(8, 2, 4, 8), ("row_0", "row_1", "col_0", "col_1"))
    placed = (P(ROW, COL), P(ROW), P(COL), P(ROW, COL), P(COL, ROW), P(ROW, COL))
    return jax.shard_map(
        shards, mesh=finer, in_specs=placed, out_specs=(P(ROW, COL), P()), check_vma=False
    )
```

```python
import jax
import jax.numpy as jnp
from jax import lax
from jax.experimental import pallas as pl
from jax.experimental.pallas import tpu as pltpu
from jax.sharding import Mesh
from jax.sharding import PartitionSpec as P

NV = 1024
NC = 1024
COUNT = NV * NC
COL = ("col_0", "col_1")
ROW = ("row_0", "row_1")
CORE_MAJOR = ("row_1", "row_0")
Z_MAJOR = ("col_1", "col_0")
EPS = 1e-06
SHIFT = 4.0
F32 = jnp.float32


def exchange(value, axis):
    return lax.all_to_all(value, axis, 0, 0, tiled=True)


def halves(value):
    upper = value.astype(jnp.bfloat16)
    return upper, (value - upper.astype(F32)).astype(jnp.bfloat16)


def dot_halves(a, b):
    (a_hi, a_lo), (b_hi, b_lo) = a, b
    return (
        jnp.dot(a_lo, b_hi, preferred_element_type=F32)
        + jnp.dot(a_hi, b_lo, preferred_element_type=F32)
        + jnp.dot(a_hi, b_hi, preferred_element_type=F32)
    )


def call(body, outs, name, smem=()):
    shapes = tuple(jax.ShapeDtypeStruct(s, F32) for s in outs)
    specs = tuple(
        pl.BlockSpec(memory_space=pltpu.SMEM if i in smem else pltpu.VMEM)
        for i in range(len(outs))
    )
    return pl.pallas_call(
        body,
        out_shape=shapes,
        out_specs=specs,
        name=name,
        compiler_params=pltpu.CompilerParams(vmem_limit_bytes=32 * 1024 * 1024),
    )


def mine(zero, one):
    return jnp.where(lax.axis_index("row_1") == 0, zero, one)


def spread_half(out, at, low, high):
    out[:, at : at + 16, :] = jnp.broadcast_to(low[None], (32, 16, 128))
    out[:, at + 16 : at + 32, :] = jnp.broadcast_to(high[None], (32, 16, 128))


def start_body(
    block_in, panel_in, valence_in, conduction_in, screened_in, packed, gap, first, pair,
    block, panel, valence, conduction, arrived,
):
    moves = [
        pltpu.make_async_copy(source, target, arrived.at[i])
        for i, (source, target) in enumerate(
            [
                (block_in, block),
                (panel_in, panel),
                (valence_in, valence),
                (conduction_in, conduction),
                (screened_in, pair.at[64:320]),
            ]
        )
    ]
    for move in moves:
        move.start()
    for move in moves[:4]:
        move.wait()
    value = jnp.concatenate([block[0:16, :], block[16:32, :]], axis=1)
    packed[...] = value
    first[:, 0:16, :] = jnp.broadcast_to(value[None], (32, 16, 128))
    half = mine(panel[0:16, :], panel[16:32, :])
    spread_half(first, 16, half[:, 0:128], half[:, 128:256])
    rows = lax.broadcasted_iota(jnp.int32, (32, 32), 0)
    lanes = lax.broadcasted_iota(jnp.int32, (32, 32), 1)
    column = jnp.sum(jnp.where(rows == lanes, conduction[...], 0.0), axis=1, keepdims=True)
    half = lax.broadcasted_iota(jnp.int32, (16, 128), 1) < 64
    upper = jnp.where(half, column[0:16], column[16:32])
    gap[...] = upper - jnp.concatenate([valence[...], valence[...]], axis=1) - SHIFT
    pair[0:32, :] = panel[:, 0:128]
    pair[32:64, :] = panel[:, 128:256]
    moves[4].wait()


def points_of(rows, panel):
    rows = halves(rows.T)
    lo = dot_halves(rows, halves(panel[:, 0].reshape(512, 128)))
    hi = dot_halves(rows, halves(panel[:, 1].reshape(512, 128)))
    return lo[0:64] + hi[64:128]


def spread_body(pair, second):
    low = mine(pair[1, 0:16, :], pair[0, 16:32, :])
    spread_half(second, 0, low, mine(pair[1, 32:48, :], pair[0, 48:64, :]))


def first_points_body(first, panel, out):
    out[...] = points_of(first[:, 0:16, :].reshape(512, 128), panel)


def second_points_body(first, y_rows, panel, out):
    x = first[:, 0:16, :].reshape(512, 128)
    y = jnp.stack([y_rows[:, at] for at in range(4)], axis=0).reshape(512, 128)
    sums = [jnp.sum(a * b, axis=0, keepdims=True) for a, b in ((x, x), (x, y), (y, y))]
    sums.append(jnp.zeros((5, 128), F32))
    image = points_of(y, panel)
    for core in range(2):
        at = 16 * core
        message = [image[at : at + 16], image[at + 32 : at + 48], *sums]
        message = jnp.concatenate(message, axis=0)
        out[core] = jnp.broadcast_to(message[None], (8, 40, 128))


def shared_panel(first, second):
    parts = [first[:, 16:32, :], first[:, 32:48, :], second[:, 0:16, :], second[:, 16:32, :]]
    return halves(jnp.concatenate([part.reshape(512, 128) for part in parts], axis=1))


def partial_points(image, first, second, out):
    points = dot_halves(halves(image.T), shared_panel(first, second)).T
    out[0] = mine(points[0:256], points[256:512])
    out[1] = mine(points[256:512], points[0:256])


def first_partial_body(image, first, second, out):
    image = mine(image[:, 0], image[:, 1]).reshape(512, 128)
    partial_points(image, first, second, out)


def second_partial_body(arrived, first, second, out, moments):
    image = jnp.stack([arrived[0, :, 0:32, :], arrived[1, :, 0:32, :]], axis=1)
    partial_points(image.reshape(512, 128), first, second, out)
    moments[...] = jnp.sum(arrived[0, :, 32:40, :] + arrived[1, :, 32:40, :], axis=0)


def weigh_body(partials, pair, first, second, out):
    zero = (partials[0, 0] + partials[1, 0]) * pair[0, 64:320, :]
    one = (partials[0, 1] + partials[1, 1]) * pair[1, 64:320, :]
    weighted = jnp.concatenate([mine(zero, one), mine(one, zero)], axis=0)
    back = dot_halves(shared_panel(first, second), halves(weighted))
    back = back.reshape(8, 2, 32, 128)
    out[0] = back[:, 0]
    out[1] = back[:, 1]


def conduct_body(parts, panel, out):
    sums = jnp.sum(parts[...], axis=1)
    back = jnp.stack([sums[0].reshape(2, 16, 128), sums[1].reshape(2, 16, 128)], axis=1)
    back = back.reshape(64, 128).T
    zero = jnp.zeros_like(back)
    lo = dot_halves(
        halves(panel[:, 0].reshape(512, 128)), halves(jnp.concatenate([back, zero], axis=1))
    )
    hi = dot_halves(
        halves(panel[:, 1].reshape(512, 128)), halves(jnp.concatenate([zero, back], axis=1))
    )
    value = (lo + hi).reshape(4, 8, 16, 128)
    for at in range(4):
        out[:, at] = value[at]


def update_body(parts, gap, x, packed, spread):
    value = gap[...] * x[...] - jnp.sum(parts[...], axis=0)
    packed[...] = value
    spread[...] = jnp.broadcast_to(value[None], spread.shape)


def total(value):
    return jnp.sum(jnp.sum(value, axis=0, keepdims=True), axis=1, keepdims=True)


def last_body(parts, gap, x, y, moments, u_out, q_out, message, scalars):
    norm = total(moments[0:1, :]) / COUNT
    inverse = 1.0 / jnp.sqrt(norm + EPS)
    first_norm = norm * inverse * inverse
    first_cross = total(moments[1:2, :]) / COUNT * inverse * inverse
    alpha = first_cross + SHIFT * first_norm
    rest = alpha - SHIFT
    beta = jnp.sqrt(
        total(moments[2:3, :]) / COUNT * inverse * inverse
        - 2.0 * rest * first_cross
        + rest * rest * first_norm
        + EPS
    )
    z = gap[...] * y[...] - jnp.sum(parts[...], axis=0)
    q_1 = x[...] * inverse
    scale = inverse / beta
    q_2 = (y[...] - rest * x[...]) * scale
    u = (z - rest * y[...]) * scale - beta * q_1
    u_out[...] = u
    q_out[...] = q_2
    lane = lax.broadcasted_iota(jnp.int32, (1, 128), 1)
    row = jnp.where(lane < 32, total(u * u), total(u * q_2))
    row = jnp.where(lane < 64, row, jnp.where(lane < 96, total(q_2 * q_2), total(q_1 * q_2)))
    message[...] = jnp.broadcast_to(row[None], message.shape)
    scalars[...] = jnp.where(lane < 64, alpha, beta)


def fold_body(parts, message):
    row = jnp.sum(parts[...], axis=0)
    message[...] = jnp.broadcast_to(row[None], message.shape)


def finish_body(parts, u, q_2, scalars, out, coefficients):
    row = jnp.sum(parts[...], axis=0) / COUNT
    uu, uq, qq, oq = row[:, 0:1], row[:, 32:33], row[:, 64:65], row[:, 96:97]
    beta_1 = scalars[:, 64:65]
    alpha = uq + beta_1 * oq + SHIFT * qq
    rest = alpha - SHIFT
    beta = jnp.sqrt(uu - 2.0 * rest * uq + rest * rest * qq + EPS)
    value = (u[...] - rest * q_2[...]) / beta
    out[0:16, :] = value[:, 0:64]
    out[16:32, :] = value[:, 64:128]
    coefficients[0] = scalars[0, 0]
    coefficients[1] = scalars[0, 64]
    coefficients[2] = alpha[0, 0]
    coefficients[3] = beta[0, 0]


def shards(excitons, valence_energy, conduction_energy, psi_valence, psi_conduction, screened):
    x, gap, first, pair = pl.pallas_call(
        start_body,
        out_shape=tuple(
            jax.ShapeDtypeStruct(shape, F32)
            for shape in [(16, 128), (16, 128), (32, 48, 128), (320, 128)]
        ),
        in_specs=[pl.BlockSpec(memory_space=pltpu.HBM)] * 5,
        out_specs=(pl.BlockSpec(memory_space=pltpu.VMEM),) * 4,
        scratch_shapes=[
            pltpu.VMEM((32, 64), F32),
            pltpu.VMEM((32, 256), F32),
            pltpu.VMEM((1, 64), F32),
            pltpu.VMEM((1, 32), F32),
            pltpu.SemaphoreType.DMA((5,)),
        ],
        name="start",
        compiler_params=pltpu.CompilerParams(vmem_limit_bytes=32 * 1024 * 1024),
    )(
        *(
            pltpu.with_memory_space_constraint(value, pltpu.HBM)
            for value in (
                excitons.T,
                psi_valence.T,
                valence_energy[None],
                conduction_energy[None],
                screened,
            )
        )
    )
    first = exchange(first, COL)
    panel_conduction = lax.all_gather(psi_conduction.T, ROW, axis=0, tiled=True)
    panel_conduction = panel_conduction.reshape(32, 2, 16, 128)

    pair = lax.all_gather(pair, "row_1", axis=0)
    (second,) = call(spread_body, [(32, 32, 128)], "spread")(pair)
    panel_conduction, second = lax.optimization_barrier((panel_conduction, second))

    def returned(partial):
        partials = lax.all_gather(partial, "row_1", axis=0)
        (back,) = call(weigh_body, [(2, 8, 32, 128)], "weigh")(
            partials, pair, first, second
        )
        back = exchange(back.reshape(16, 32, 128), CORE_MAJOR).reshape(2, 8, 32, 128)
        (kernel,) = call(conduct_body, [(8, 4, 16, 128)], "conduct")(back, panel_conduction)
        return exchange(kernel.reshape(32, 16, 128), Z_MAJOR)

    (image,) = call(first_points_body, [(64, 128)], "points_one")(first, panel_conduction)
    image, second = lax.optimization_barrier((image, second))
    second = exchange(second, COL)
    image = lax.all_gather(image, ROW, axis=0, tiled=True).reshape(32, 2, 16, 128)
    (partial,) = call(first_partial_body, [(2, 256, 128)], "partial_one")(image, first, second)
    y, spread = call(update_body, [(16, 128), (32, 16, 128)], "update")(returned(partial), gap, x)

    y_rows = exchange(spread, Z_MAJOR).reshape(8, 4, 16, 128)
    (image,) = call(second_points_body, [(2, 8, 40, 128)], "points_two")(
        first, y_rows, panel_conduction
    )
    image = exchange(image.reshape(16, 40, 128), CORE_MAJOR).reshape(2, 8, 40, 128)
    partial, moments = call(second_partial_body, [(2, 256, 128), (8, 128)], "partial_two")(
        image, first, second
    )
    u, q_2, message, scalars = call(
        last_body, [(16, 128), (16, 128), (64, 1, 128), (1, 128)], "last"
    )(returned(partial), gap, x, y, moments)
    (message,) = call(fold_body, [(8, 1, 128)], "fold")(exchange(message, ("col_0", *CORE_MAJOR)))
    out, coefficients = call(finish_body, [(32, 64), (4,)], "finish", smem=(1,))(
        exchange(message, "col_1"), u, q_2, scalars
    )
    return out.T, coefficients


def solution(mesh):
    finer = Mesh(mesh.devices.reshape(8, 2, 4, 8), ("row_0", "row_1", "col_0", "col_1"))
    placed = (P(ROW, COL), P(ROW), P(COL), P(ROW, COL), P(COL, ROW), P(ROW, COL))
    return jax.shard_map(
        shards, mesh=finer, in_specs=placed, out_specs=(P(ROW, COL), P()), check_vma=False
    )
```
